32 devices in a mesh: gz: 8 (over z, y), gy: 4 (over x, core).
Axes of the slice: x: 2, y: 2, z: 4, core: 2. Of those that a mesh axis runs over, the one named last changes fastest.
Arguments:
- velocity: float32 [2, 6, 1024, 2048], P(None, None, 'gy', 'gz'), may hold values from -6 to 6
Outputs:
- spectrum: float32 [2, 6, 1024, 2048], P(None, None, 'gy', 'gz')
The draws below stay inside these ranges and needn't reach their ends.
All inputs are finite; a program needn't handle non-finite values.
Results may differ from the reference program's by a relative error of at most 0.000098.
Values sent between devices are 32-bit elements; how exact they have to be, the bound alone decides.
No kernel may reach another device: no remote copies, remote signals or barrier semaphores. Data moves between devices by JAX's collectives and lax.ppermute only.
A program may use at most 64 MiB of HBM per device.

```python
import jax
import jax.numpy as jnp
import numpy as np
from jax import lax

PLANES = 6
NY = 1024
NZ = 2048
N_GZ = 8
N_GY = 4


def level_of(rng, dims, pieces, low, high):
    def one(axis_at, blocks):
        draws = jax.random.uniform(jax.random.fold_in(jax.random.fold_in(rng, 6), axis_at), (blocks,), jnp.float32, low / len(pieces), high / len(pieces))
        return jnp.repeat(jnp.exp(draws), dims[axis_at] // blocks).reshape((-1,) + (1,) * (len(dims) - axis_at - 1))

    gain = one(*pieces[0])
    for cut in pieces[1:]:
        gain = gain * one(*cut)
    return gain


def scatter_about(own_key, extent, scale, bound, cuts=(), kind=jnp.bfloat16):
    drawn = scale * jax.random.normal(own_key, extent, jnp.float32)
    if cuts:
        drawn = drawn * level_of(own_key, extent, cuts, -0.22, 0.18)
    return jnp.clip(drawn, -bound, bound).astype(kind)


def setup_inputs(seed: int = 0) -> dict:
    splits = jax.random.split(jax.random.key(seed), 2)
    velocity = scatter_about(splits[0], (2, PLANES, NY, NZ), 1.0, 6.0, ((2, 4), (3, 8)), jnp.float32)
    return {"velocity": velocity}


def reversed_order(device_count):
    bit_count = device_count.bit_length() - 1
    result = []
    for column in range(device_count):
        value = 0
        for place in range(bit_count):
            value += ((column >> place) & 1) << (bit_count - 1 - place)
        result.append(value)
    return np.array(result, dtype=np.int32)


def reorder_axis(complex_field, axis_number, device_count):
    moved = jnp.moveaxis(complex_field, axis_number, -1)
    length = moved.shape[-1]
    local_len = length // device_count
    split = moved.reshape(moved.shape[:-1] + (local_len, device_count))
    split = jnp.swapaxes(split, -1, -2)
    split = jnp.take(split, jnp.asarray(reversed_order(device_count)), axis=-2)
    placed = split.reshape(moved.shape)
    return jnp.moveaxis(placed, -1, axis_number)


def reference(velocity):
    complex_field = lax.complex(velocity[0], velocity[1])
    transformed = jnp.fft.fft(complex_field, axis=-1, norm="ortho")
    transformed = jnp.fft.fft(transformed, axis=-2, norm="ortho")
    transformed = reorder_axis(transformed, 2, N_GZ)
    transformed = reorder_axis(transformed, 1, N_GY)
    return jnp.stack([jnp.real(transformed), jnp.imag(transformed)]).astype(jnp.float32)
```

```python
import functools
import math

import jax
import jax.numpy as jnp
from jax import lax
from jax.experimental import pallas as pl
from jax.experimental.pallas import tpu as pltpu
from jax.sharding import PartitionSpec as P


F32 = jnp.float32
BF16 = jnp.bfloat16
SMEM = pl.BlockSpec(memory_space=pltpu.SMEM)


def exchanged(block, axis, mask):
    count = lax.axis_size(axis)
    return lax.ppermute(block, axis, [(i, i ^ mask) for i in range(count)])


def reversed_bits(index, bit_count):
    result = index * 0
    for place in range(bit_count):
        result = result + ((index >> place) & 1) * 2 ** (bit_count - 1 - place)
    return result


def unit(products, length):
    phase = -2.0 * math.pi * (products % length).astype(F32) / length
    return jnp.cos(phase), jnp.sin(phase)


def rows_of(part, quarter):
    return pl.ds(pl.multiple_of(part * quarter, quarter), quarter)


def params(step_bytes):
    return pltpu.CompilerParams(dimension_semantics=("arbitrary",))


def estimate(flops, count):
    return pl.CostEstimate(flops=flops, transcendentals=0, bytes_accessed=4 * count)


def dft_matrix(frequency, count, local):
    length = count * local
    at = jnp.arange(local, dtype=jnp.int32)
    cosine, sine = unit(at[:, None] * (frequency + count * at[None, :]), length)
    scale = 1.0 / math.sqrt(length)
    return cosine * scale, sine * scale


def split(values):
    high = lax.reduce_precision(values, 8, 7)
    return jnp.stack([high.astype(BF16), (values - high).astype(BF16)])


def right_matrix(frequency, count, local):
    cosine, sine = dft_matrix(frequency, count, local)
    return split(jnp.block([[cosine, sine], [-sine, cosine]]))


def left_matrix(frequency, count, local):
    cosine, sine = dft_matrix(frequency, count, local)
    return split(jnp.block([[cosine.T, -sine.T], [sine.T, cosine.T]]))


def halves(values):
    high = values.astype(BF16)
    return high, (values - high.astype(F32)).astype(BF16)


def dot3(left, right):
    def single(a, b):
        return jnp.dot(a, b, preferred_element_type=F32)

    return single(left[0], right[0]) + (single(left[1], right[0]) + single(left[0], right[1]))


def along_last(real, imag, matrix_ref):
    local = real.shape[-1]
    mixed = dot3(halves(jnp.concatenate([real, imag], axis=1)), (matrix_ref[0], matrix_ref[1]))
    return mixed[:, :local], mixed[:, local:]


def along_first(real, imag, matrix_ref):
    local = real.shape[0]
    mixed = dot3((matrix_ref[0], matrix_ref[1]), halves(jnp.concatenate([real, imag], axis=0)))
    return mixed[:local], mixed[local:]


def pack_kernel(index_ref, x_ref, *out_refs):
    quarter = out_refs[0].shape[2]
    for step, out_ref in enumerate(out_refs):
        out_ref[...] = x_ref[:, :, rows_of(index_ref[0] ^ (step + 1), quarter), :]


def pack(x, part, start, planes):
    _, _, rows, columns = x.shape
    quarter = rows // 4
    piece = jax.ShapeDtypeStruct((2, planes, quarter, columns), F32)
    return pl.pallas_call(
        pack_kernel,
        grid=(planes,),
        in_specs=[SMEM, pl.BlockSpec((2, 1, rows, columns), lambda i: (0, start + i, 0, 0))],
        out_specs=[pl.BlockSpec((2, 1, quarter, columns), lambda i: (0, i, 0, 0))] * 3,
        out_shape=[piece] * 3,
        cost_estimate=estimate(0, 14 * planes * quarter * columns),
        name="pack",
    )(part, x)


def mix_kernel(index_ref, coef_ref, x_ref, r1_ref, r2_ref, r3_ref, out_ref):
    quarter = out_ref.shape[3]
    own = x_ref[:, 0, rows_of(index_ref[0], quarter), :]
    pieces = [own, r1_ref[:, 0], r2_ref[:, 0], r3_ref[:, 0]]
    for e in range(4):
        real, imag = None, None
        for d in range(4):
            c, s = coef_ref[0, 4 * e + d], coef_ref[1, 4 * e + d]
            a, b = pieces[d][0], pieces[d][1]
            re, im = a * c - b * s, a * s + b * c
            real = re if real is None else real + re
            imag = im if imag is None else imag + im
        out_ref[e, 0, 0] = real
        out_ref[e, 1, 0] = imag


def mix(x, start, received, part, coefs):
    _, planes, quarter, columns = received[0].shape
    rows = x.shape[2]
    small = pl.BlockSpec((2, 1, quarter, columns), lambda i: (0, i, 0, 0))
    return pl.pallas_call(
        mix_kernel,
        grid=(planes,),
        in_specs=[SMEM, SMEM, pl.BlockSpec((2, 1, rows, columns), lambda i: (0, start + i, 0, 0))] + [small] * 3,
        out_specs=pl.BlockSpec((4, 2, 1, quarter, columns), lambda i: (0, 0, i, 0, 0)),
        out_shape=jax.ShapeDtypeStruct((4, 2, planes, quarter, columns), F32),
        cost_estimate=estimate(128 * planes * quarter * columns, 22 * planes * quarter * columns),
        name="mix",
    )(part, coefs, x, *received)


def joined(own, other, coef_ref):
    flip, c, s = coef_ref[0], coef_ref[1], coef_ref[2]
    real = own[0] * flip + other[0]
    imag = own[1] * flip + other[1]
    return real * c - imag * s, real * s + imag * c


def butterfly_kernel(coef_ref, own_ref, other_ref, *out_refs):
    for e in range(own_ref.shape[0]):
        real, imag = joined(own_ref[e, :, 0], other_ref[e, :, 0], coef_ref)
        if len(out_refs) == 1:
            out_refs[0][e, 0, 0] = real
            out_refs[0][e, 1, 0] = imag
        else:
            out_refs[e][0, 0] = real
            out_refs[e][1, 0] = imag


def butterfly(own, other, coefs, start=0, apart=False):
    groups = own.shape[0]
    _, _, planes, rows, columns = other.shape
    block = (groups, 2, 1, rows, columns)
    if apart:
        out_specs = [pl.BlockSpec((2, 1, rows, columns), lambda i: (0, i, 0, 0))] * groups
        out_shape = [jax.ShapeDtypeStruct((2, planes, rows, columns), F32)] * groups
    else:
        out_specs = pl.BlockSpec(block, lambda i: (0, 0, i, 0, 0))
        out_shape = jax.ShapeDtypeStruct(other.shape, F32)
    return pl.pallas_call(
        butterfly_kernel,
        grid=(planes,),
        in_specs=[
            SMEM,
            pl.BlockSpec(block, lambda i: (0, 0, start + i, 0, 0)),
            pl.BlockSpec(block, lambda i: (0, 0, i, 0, 0)),
        ],
        out_specs=out_specs,
        out_shape=out_shape,
        cost_estimate=estimate(5 * other.size, 3 * other.size),
        name="butterfly",
    )(coefs, own, other)


def finish_kernel(index_ref, right_ref, left_ref, e0_ref, e1_ref, e2_ref, e3_ref, *rest):
    out_ref, whole = rest[-2], rest[-1]
    quarter = e0_ref.shape[2]
    for d, ref in enumerate((e0_ref, e1_ref, e2_ref, e3_ref)):
        whole[:, rows_of(index_ref[0] ^ d, quarter), :] = ref[:, 0]
    real, imag = along_last(whole[0], whole[1], right_ref)
    real, imag = along_first(real, imag, left_ref)
    out_ref[0, 0] = real
    out_ref[1, 0] = imag


def finish(pieces, part, right, left, out, start, total):
    _, planes, quarter, columns = pieces[0].shape
    rows = 4 * quarter
    small = pl.BlockSpec((2, 1, quarter, columns), lambda i: (0, i, 0, 0))
    whole = pl.BlockSpec((2, 2 * columns, 2 * columns), lambda i: (0, 0, 0))
    whole_left = pl.BlockSpec((2, 2 * rows, 2 * rows), lambda i: (0, 0, 0))
    in_specs = [SMEM, whole, whole_left] + [small] * 4
    args = [part, right, left, *pieces]
    aliases = {}
    if out is not None:
        in_specs.append(pl.BlockSpec(memory_space=pl.ANY))
        aliases = {len(args): 0}
        args.append(out)
    return pl.pallas_call(
        finish_kernel,
        grid=(planes,),
        in_specs=in_specs,
        out_specs=pl.BlockSpec((2, 1, rows, columns), lambda i: (0, start + i, 0, 0)),
        out_shape=jax.ShapeDtypeStruct((2, total, rows, columns), F32),
        scratch_shapes=[pltpu.VMEM((2, rows, columns), F32)],
        input_output_aliases=aliases,
        cost_estimate=estimate(24 * planes * rows * columns * (rows + columns), 4 * planes * rows * columns),
        name="finish",
    )(*args)


def pair_coefs(index, bit):
    upper = (index >> bit) & 1
    lower = index % 2**bit
    cosine, sine = unit(lower * upper, 2 ** (bit + 1))
    return jnp.stack([(1 - 2 * upper).astype(F32), cosine, sine])


def mix_coefs(part, rest, count):
    step = jnp.arange(4, dtype=jnp.int32)
    k = reversed_bits(part ^ step, 2)[:, None]
    d = (part ^ step)[None, :]
    cosine, sine = unit(rest * k + (count // 4) * (d * k), count)
    return jnp.stack([cosine.reshape(-1), sine.reshape(-1)])


def chunks_of(planes):
    size = max(1, planes // 3)
    starts = list(range(0, planes, size))
    return [(at, min(size, planes - at)) for at in starts]


def shards(velocity):
    _, planes, rows, columns = velocity.shape
    z_count = lax.axis_size("gz")
    y_count = lax.axis_size("gy")
    z_bits = z_count.bit_length() - 1
    y_bits = y_count.bit_length() - 1
    z_index = lax.axis_index("gz")
    y_index = lax.axis_index("gy")
    stride = z_count // 4
    part = z_index // stride
    part_arg = part.reshape(1)
    coefs = mix_coefs(part, z_index % stride, z_count)
    right = right_matrix(reversed_bits(z_index, z_bits), z_count, columns)
    left = left_matrix(reversed_bits(y_index, y_bits), y_count, rows)
    z_pairs = [("gz", bit, pair_coefs(z_index, bit)) for bit in reversed(range(z_bits - 2))]
    y_pairs = [("gy", bit, pair_coefs(y_index, bit)) for bit in reversed(range(y_bits))]

    def run_pairs(own, pairs, start=0, apart=False, size=None):
        for at, (axis, bit, pair) in enumerate(pairs):
            sent = own
            if size is not None and own.shape[2] != size:
                sent = own[:, :, start : start + size]
            other = exchanged(sent, axis, 2**bit)
            last = apart and at == len(pairs) - 1
            own = butterfly(own, other, pair, start if own.shape[2] != other.shape[2] else 0, last)
        return own

    chunks = chunks_of(planes)
    result = None
    for number, (start, size) in enumerate(chunks):
        early = number == len(chunks) - 1
        if early:
            data = run_pairs(velocity[None], y_pairs, start, size=size)[0]
            data_start = 0
            pairs = z_pairs
        else:
            data, data_start = velocity, start
            pairs = z_pairs + y_pairs
        sent = pack(data, part_arg, data_start, size)
        received = [exchanged(piece, "gz", (d + 1) * stride) for d, piece in enumerate(sent)]
        mixed = mix(data, data_start, received, part_arg, coefs)
        pieces = run_pairs(mixed, pairs, apart=True)
        if not pairs:
            pieces = [pieces[e] for e in range(4)]
        back = [pieces[0]] + [exchanged(pieces[d], "gz", d * stride) for d in range(1, 4)]
        result = finish(back, part_arg, right, left, result, start, planes)
    return result


def solution(mesh):
    in_specs = (P(None, None, "gy", "gz"),)
    out_specs = P(None, None, "gy", "gz")
    return jax.shard_map(shards, mesh=mesh, in_specs=in_specs, out_specs=out_specs, check_vma=False)
```

```python
import functools
import math

import jax
import jax.numpy as jnp
from jax import lax
from jax.experimental import pallas as pl
from jax.experimental.pallas import tpu as pltpu
from jax.sharding import PartitionSpec as P


F32 = jnp.float32
BF16 = jnp.bfloat16
SMEM = pl.BlockSpec(memory_space=pltpu.SMEM)
VMEM = pl.BlockSpec(memory_space=pltpu.VMEM)
ANY = pl.BlockSpec(memory_space=pl.ANY)


def exchanged(block, axis, mask):
    count = lax.axis_size(axis)
    return lax.ppermute(block, axis, [(i, i ^ mask) for i in range(count)])


def reversed_bits(index, bit_count):
    result = index * 0
    for place in range(bit_count):
        result = result + ((index >> place) & 1) * 2 ** (bit_count - 1 - place)
    return result


def unit(products, length):
    phase = -2.0 * math.pi * (products % length).astype(F32) / length
    return jnp.cos(phase), jnp.sin(phase)


def rows_of(part, quarter):
    return pl.ds(pl.multiple_of(part * quarter, quarter), quarter)


def estimate(flops, count):
    return pl.CostEstimate(flops=flops, transcendentals=0, bytes_accessed=4 * count)


def dft_matrix(frequency, count, local):
    length = count * local
    at = jnp.arange(local, dtype=jnp.int32)
    cosine, sine = unit(at[:, None] * (frequency + count * at[None, :]), length)
    scale = 1.0 / math.sqrt(length)
    return cosine * scale, sine * scale


def split(values):
    high = lax.reduce_precision(values, 8, 7)
    return jnp.stack([high.astype(BF16), (values - high).astype(BF16)])


def right_matrix(frequency, count, local):
    cosine, sine = dft_matrix(frequency, count, local)
    return split(jnp.block([[cosine, sine], [-sine, cosine]]))


def left_matrix(frequency, count, local):
    cosine, sine = dft_matrix(frequency, count, local)
    return split(jnp.block([[cosine.T, -sine.T], [sine.T, cosine.T]]))


def halves(values):
    high = values.astype(BF16)
    return high, (values - high.astype(F32)).astype(BF16)


def dot3(left, right):
    def single(a, b):
        return jnp.dot(a, b, preferred_element_type=F32)

    return single(left[0], right[0]) + (single(left[1], right[0]) + single(left[0], right[1]))


def along_last(real, imag, matrix_ref):
    local = real.shape[-1]
    mixed = dot3(halves(jnp.concatenate([real, imag], axis=1)), (matrix_ref[0], matrix_ref[1]))
    return mixed[:, :local], mixed[:, local:]


def along_first(real, imag, matrix_ref):
    local = real.shape[0]
    mixed = dot3((matrix_ref[0], matrix_ref[1]), halves(jnp.concatenate([real, imag], axis=0)))
    return mixed[:local], mixed[local:]


def per_rows(planes, rows, step, body):
    def one(at, carry):
        body(at // (rows // step), pl.ds(pl.multiple_of(at % (rows // step) * step, step), step))
        return carry

    lax.fori_loop(0, planes * (rows // step), one, 0, unroll=2)


def pack_kernel(chunks, index_ref, x_ref, *refs):
    sems = refs[-1]
    quarter = refs[0].shape[2]
    copies = []
    for number, (start, size) in enumerate(chunks):
        for d in (1, 2, 3, 0):
            source = x_ref.at[:, pl.ds(start, size), rows_of(index_ref[0] ^ d, quarter), :]
            at = 4 * number + d
            copies.append(pltpu.make_async_copy(source, refs[at], sems.at[at]))
    for copy in copies:
        copy.start()
    for copy in copies:
        copy.wait()


def pack(x, part, chunks):
    _, _, rows, columns = x.shape
    quarter = rows // 4
    shapes, specs = [], []
    for _, size in chunks:
        shapes += [jax.ShapeDtypeStruct((2, size, quarter, columns), F32)] * 4
        specs += [VMEM, ANY, ANY, ANY]
    total = sum(size for _, size in chunks)
    outs = pl.pallas_call(
        functools.partial(pack_kernel, chunks),
        in_specs=[SMEM, ANY],
        out_specs=specs,
        out_shape=shapes,
        scratch_shapes=[pltpu.SemaphoreType.DMA((len(shapes),))],
        cost_estimate=estimate(0, 16 * total * quarter * columns),
        name="pack",
    )(part, x)
    return [outs[4 * i : 4 * i + 4] for i in range(len(chunks))]


def mix_kernel(coef_ref, *refs):
    pieces, outs = refs[:4], refs[4:]
    planes, half = outs[0].shape[2:4]
    for h, out_ref in enumerate(outs):

        def body(plane, at):
            rows = pl.ds(pl.multiple_of(h * half + at.start, 8), at.size)
            values = [(ref[0, plane, rows, :], ref[1, plane, rows, :]) for ref in pieces]
            for e in range(4):
                real, imag = None, None
                for d in range(4):
                    c, s = coef_ref[0, 4 * e + d], coef_ref[1, 4 * e + d]
                    a, b = values[d]
                    re, im = a * c - b * s, a * s + b * c
                    real = re if real is None else real + re
                    imag = im if imag is None else imag + im
                out_ref[e, 0, plane, at, :] = real
                out_ref[e, 1, plane, at, :] = imag

        per_rows(planes, half, 8, body)


def mix(pieces, coefs):
    _, planes, quarter, columns = pieces[0].shape
    half = jax.ShapeDtypeStruct((4, 2, planes, quarter // 2, columns), F32)
    return pl.pallas_call(
        mix_kernel,
        in_specs=[SMEM] + [VMEM] * 4,
        out_specs=[VMEM] * 2,
        out_shape=[half] * 2,
        cost_estimate=estimate(128 * planes * quarter * columns, 16 * planes * quarter * columns),
        name="mix",
    )(coefs, *pieces)


def joined(own, other, coefs):
    flip, c, s = coefs
    real = own[0] * flip + other[0]
    imag = own[1] * flip + other[1]
    return real * c - imag * s, real * s + imag * c


def butterfly_kernel(kinds, coef_ref, *refs):
    count = len(kinds)
    for h, (first, apart) in enumerate(kinds):
        own_ref, other_ref, outs = refs[2 * h], refs[2 * h + 1], refs[2 * count :]
        groups, _, planes, rows, _ = own_ref.shape
        coefs = coef_ref[h, 0], coef_ref[h, 1], coef_ref[h, 2]

        def body(plane, at):
            into = pl.ds(pl.multiple_of(first + at.start, 8), at.size)
            for e in range(groups):
                own = own_ref[e, 0, plane, at, :], own_ref[e, 1, plane, at, :]
                other = other_ref[e, 0, plane, at, :], other_ref[e, 1, plane, at, :]
                real, imag = joined(own, other, coefs)
                if apart:
                    outs[e][0, plane, into, :] = real
                    outs[e][1, plane, into, :] = imag
                else:
                    out_ref = outs[h if len(outs) > 1 else 0]
                    out_ref[e, 0, plane, into, :] = real
                    out_ref[e, 1, plane, into, :] = imag

        per_rows(planes, rows, 8, body)


def butterfly(blocks, coefs, form):
    own = blocks[0][0]
    groups, _, planes, rows, columns = own.shape
    total = rows * len(blocks)
    if form == "same":
        shapes = [own] * len(blocks)
        kinds = tuple((0, False) for _ in blocks)
    elif form == "whole":
        shapes = [jax.ShapeDtypeStruct((groups, 2, planes, total, columns), F32)]
        kinds = tuple((h * rows, False) for h in range(len(blocks)))
    else:
        shapes = [jax.ShapeDtypeStruct((2, planes, total, columns), F32)] * groups
        kinds = tuple((h * rows, True) for h in range(len(blocks)))
    return pl.pallas_call(
        functools.partial(butterfly_kernel, kinds),
        in_specs=[SMEM] + [VMEM] * (2 * len(blocks)),
        out_specs=[VMEM] * len(shapes),
        out_shape=[jax.ShapeDtypeStruct(shape.shape, F32) for shape in shapes],
        cost_estimate=estimate(5 * own.size * len(blocks), 3 * own.size * len(blocks)),
        name="butterfly",
    )(jnp.stack(coefs), *[array for pair in blocks for array in pair])


def finish_kernel(start, index_ref, right_ref, left_ref, e0_ref, e1_ref, e2_ref, e3_ref, *rest):
    out_ref, whole, done, sems = rest[-4:]
    _, planes, quarter, _ = e0_ref.shape
    copies = []
    for plane in range(planes):
        for d, ref in enumerate((e0_ref, e1_ref, e2_ref, e3_ref)):
            whole[plane, :, rows_of(index_ref[0] ^ d, quarter), :] = ref[:, plane]
        real, imag = along_last(whole[plane, 0], whole[plane, 1], right_ref)
        real, imag = along_first(real, imag, left_ref)
        done[plane, 0] = real
        done[plane, 1] = imag
        copies.append(pltpu.make_async_copy(done.at[plane], out_ref.at[:, start + plane], sems.at[plane]))
        copies[-1].start()
    for copy in copies:
        copy.wait()


def finish(pieces, part, right, left, out, start, total):
    _, planes, quarter, columns = pieces[0].shape
    rows = 4 * quarter
    in_specs = [SMEM] + [VMEM] * 6
    args = [part, right, left, *pieces]
    aliases = {}
    if out is not None:
        in_specs.append(ANY)
        aliases = {len(args): 0}
        args.append(out)
    return pl.pallas_call(
        functools.partial(finish_kernel, start),
        in_specs=in_specs,
        out_specs=ANY,
        out_shape=jax.ShapeDtypeStruct((2, total, rows, columns), F32),
        scratch_shapes=[
            pltpu.VMEM((planes, 2, rows, columns), F32),
            pltpu.VMEM((planes, 2, rows, columns), F32),
            pltpu.SemaphoreType.DMA((planes,)),
        ],
        input_output_aliases=aliases,
        cost_estimate=estimate(24 * planes * rows * columns * (rows + columns), 4 * planes * rows * columns),
        name="finish",
    )(*args)


def pair_coefs(index, bit):
    upper = (index >> bit) & 1
    lower = index % 2**bit
    cosine, sine = unit(lower * upper, 2 ** (bit + 1))
    return jnp.stack([(1 - 2 * upper).astype(F32), cosine, sine])


def mix_coefs(part, rest, count):
    step = jnp.arange(4, dtype=jnp.int32)
    k = reversed_bits(part ^ step, 2)[:, None]
    d = (part ^ step)[None, :]
    cosine, sine = unit(rest * k + (count // 4) * (d * k), count)
    return jnp.stack([cosine.reshape(-1), sine.reshape(-1)])


def chunks_of(planes):
    size = max(1, planes // 3)
    starts = list(range(0, planes, size))
    return [(at, min(size, planes - at)) for at in starts]


def shards(velocity):
    _, planes, rows, columns = velocity.shape
    z_count = lax.axis_size("gz")
    y_count = lax.axis_size("gy")
    z_bits = z_count.bit_length() - 1
    y_bits = y_count.bit_length() - 1
    z_index = lax.axis_index("gz")
    y_index = lax.axis_index("gy")
    stride = z_count // 4
    part = z_index // stride
    part_arg = part.reshape(1)
    coefs = mix_coefs(part, z_index % stride, z_count)
    right = right_matrix(reversed_bits(z_index, z_bits), z_count, columns)
    left = left_matrix(reversed_bits(y_index, y_bits), y_count, rows)
    z_pairs = [("gz", bit, pair_coefs(z_index, bit)) for bit in reversed(range(z_bits - 2))]
    y_pairs = [("gy", bit, pair_coefs(y_index, bit)) for bit in reversed(range(y_bits))]
    ways = list(zip(z_pairs + y_pairs[:-1], y_pairs[:-1] + z_pairs))
    axis, bit, last = y_pairs[-1]

    chunks = chunks_of(planes)
    packed = []
    for group in (chunks[:1], chunks[1:]):
        packed += pack(velocity, part_arg, group)
    received = []
    for own, *sent in packed:
        received.append([own] + [exchanged(piece, "gz", (d + 1) * stride) for d, piece in enumerate(sent)])
    result = None
    for (start, size), pieces in zip(chunks, received):
        now = mix(pieces, coefs)
        for step, way in enumerate(ways):
            blocks = [(own, exchanged(own, pair[0], 2 ** pair[1])) for own, pair in zip(now, way)]
            form = "whole" if step == len(ways) - 1 else "same"
            now = butterfly(blocks, [pair[2] for pair in way], form)
        pieces = butterfly([(now[0], exchanged(now[0], axis, 2**bit))], [last], "apart")
        back = [pieces[0]] + [exchanged(pieces[d], "gz", d * stride) for d in range(1, 4)]
        result = finish(back, part_arg, right, left, result, start, planes)
    return result


def solution(mesh):
    in_specs = (P(None, None, "gy", "gz"),)
    out_specs = P(None, None, "gy", "gz")
    return jax.shard_map(shards, mesh=mesh, in_specs=in_specs, out_specs=out_specs, check_vma=False)
```

```python
import functools
import math

import jax
import jax.numpy as jnp
from jax import lax
from jax.experimental import pallas as pl
from jax.experimental.pallas import tpu as pltpu
from jax.sharding import PartitionSpec as P


F32 = jnp.float32
BF16 = jnp.bfloat16
SMEM = pl.BlockSpec(memory_space=pltpu.SMEM)
VMEM = pl.BlockSpec(memory_space=pltpu.VMEM)
ANY = pl.BlockSpec(memory_space=pl.ANY)


def exchanged(block, axis, mask):
    count = lax.axis_size(axis)
    return lax.ppermute(block, axis, [(i, i ^ mask) for i in range(count)])


def reversed_bits(index, bit_count):
    result = index * 0
    for place in range(bit_count):
        result = result + ((index >> place) & 1) * 2 ** (bit_count - 1 - place)
    return result


def unit(products, length):
    phase = -2.0 * math.pi * (products % length).astype(F32) / length
    return jnp.cos(phase), jnp.sin(phase)


def estimate(flops, count):
    return pl.CostEstimate(flops=flops, transcendentals=0, bytes_accessed=4 * count)


def dft_matrix(frequency, count, local, at):
    length = count * local
    to = jnp.arange(local, dtype=jnp.int32)
    cosine, sine = unit(at[:, None] * (frequency + count * to[None, :]), length)
    scale = 1.0 / math.sqrt(length)
    return cosine * scale, sine * scale


def split(values):
    high = lax.reduce_precision(values, 8, 7)
    return jnp.stack([high.astype(BF16), (values - high).astype(BF16)])


def right_matrix(frequency, count, local):
    cosine, sine = dft_matrix(frequency, count, local, jnp.arange(local, dtype=jnp.int32))
    return split(jnp.block([[cosine, sine], [-sine, cosine]]))


def left_matrix(frequency, count, local, part):
    at = jnp.arange(local, dtype=jnp.int32)
    quarter = local // 4
    at = (part ^ (at // quarter)) * quarter + at % quarter
    cosine, sine = dft_matrix(frequency, count, local, at)
    return split(jnp.block([[cosine.T, -sine.T], [sine.T, cosine.T]]))


def halves(values):
    high = values.astype(BF16)
    return high, (values - high.astype(F32)).astype(BF16)


def dot3(left, right):
    def single(a, b):
        return jnp.dot(a, b, preferred_element_type=F32)

    return single(left[0], right[0]) + (single(left[1], right[0]) + single(left[0], right[1]))


def along_last(real, imag, matrix_ref):
    local = real.shape[-1]
    mixed = dot3(halves(jnp.concatenate([real, imag], axis=1)), (matrix_ref[0], matrix_ref[1]))
    return mixed[:, :local], mixed[:, local:]


def along_first(real, imag, matrix_ref):
    local = real.shape[0]
    mixed = dot3((matrix_ref[0], matrix_ref[1]), halves(jnp.concatenate([real, imag], axis=0)))
    return mixed[:local], mixed[local:]


def after(value, done):
    return value if done is None else lax.optimization_barrier((value, done))[0]


def turned(values, cosine, sine):
    sign = jnp.array([-1.0, 1.0], F32).reshape(2, 1, 1, 1)
    return values * cosine + jnp.flip(values, -4) * (sign * sine)


def mixed(pieces, coefs):
    total = None
    for d, piece in enumerate(pieces):
        term = turned(piece[None], coefs[0, :, d].reshape(4, 1, 1, 1, 1), coefs[1, :, d].reshape(4, 1, 1, 1, 1))
        total = term if total is None else total + term
    return total


def butterfly(own, other, pair):
    flip, twist = pair
    both = own * flip + other
    return both if twist is None else turned(both, *twist)


def finish_kernel(start, right_ref, left_ref, e0_ref, e1_ref, e2_ref, e3_ref, *rest):
    out_ref, done, sems = rest[-3:]
    planes = e0_ref.shape[1]
    copies = []
    for plane in range(planes):
        refs = (e0_ref, e1_ref, e2_ref, e3_ref)
        whole = [jnp.concatenate([ref[part, plane] for ref in refs], axis=0) for part in range(2)]
        real, imag = along_last(whole[0], whole[1], right_ref)
        real, imag = along_first(real, imag, left_ref)
        done[plane, 0] = real
        done[plane, 1] = imag
        copies.append(pltpu.make_async_copy(done.at[plane], out_ref.at[:, start + plane], sems.at[plane]))
        copies[-1].start()
    for copy in copies:
        copy.wait()


def finish(pieces, right, left, out, start, total):
    _, planes, quarter, columns = pieces[0].shape
    rows = 4 * quarter
    in_specs = [VMEM] * 6
    args = [right, left, *pieces]
    aliases = {}
    if out is not None:
        in_specs.append(ANY)
        aliases = {len(args): 0}
        args.append(out)
    return pl.pallas_call(
        functools.partial(finish_kernel, start),
        in_specs=in_specs,
        out_specs=ANY,
        out_shape=jax.ShapeDtypeStruct((2, total, rows, columns), F32),
        scratch_shapes=[
            pltpu.VMEM((planes, 2, rows, columns), F32),
            pltpu.SemaphoreType.DMA((planes,)),
        ],
        input_output_aliases=aliases,
        cost_estimate=estimate(24 * planes * rows * columns * (rows + columns), 4 * planes * rows * columns),
        name="finish",
    )(*args)


def pair_of(axis, index, bit):
    upper = (index >> bit) & 1
    lower = index % 2**bit
    flip = (1 - 2 * upper).astype(F32)
    return axis, 2**bit, (flip, unit(lower * upper, 2 ** (bit + 1)) if bit else None)


def mix_coefs(part, rest, count):
    step = jnp.arange(4, dtype=jnp.int32)
    k = reversed_bits(part ^ step, 2)[:, None]
    d = (part ^ step)[None, :]
    return jnp.stack(unit(rest * k + (count // 4) * (d * k), count))


def chunks_of(planes):
    size = max(1, planes // 3)
    starts = list(range(0, planes, size))
    return [(at, min(size, planes - at)) for at in starts]


def shards(velocity):
    _, planes, rows, columns = velocity.shape
    z_count = lax.axis_size("gz")
    y_count = lax.axis_size("gy")
    z_bits = z_count.bit_length() - 1
    y_bits = y_count.bit_length() - 1
    z_index = lax.axis_index("gz")
    y_index = lax.axis_index("gy")
    stride = z_count // 4
    part = z_index // stride
    quarter = rows // 4
    coefs = mix_coefs(part, z_index % stride, z_count)
    right = right_matrix(reversed_bits(z_index, z_bits), z_count, columns)
    left = left_matrix(reversed_bits(y_index, y_bits), y_count, rows, part)
    z_pairs = [pair_of("gz", z_index, bit) for bit in reversed(range(z_bits - 2))]
    y_pairs = [pair_of("gy", y_index, bit) for bit in reversed(range(y_bits))]
    ways = list(zip(z_pairs + y_pairs[:-1], y_pairs[:-1] + z_pairs))
    ways.append((y_pairs[-1], y_pairs[-1]))

    chunks = chunks_of(planes)
    quarters = velocity.reshape(2, planes, 4, quarter, columns)
    received = []
    for start, size in chunks:
        mine = quarters[:, start : start + size]
        pieces = [lax.dynamic_index_in_dim(mine, part ^ d, 2, False) for d in range(4)]
        received.append(pieces[:1] + [exchanged(pieces[d], "gz", d * stride) for d in range(1, 4)])

    state = [None] * len(chunks)
    done = None

    def mix_step(i):
        cut = quarter // 2
        sides = [[piece[:, :, at : at + cut] for piece in received[i]] for at in (0, cut)]
        return [mixed(after(side, done), coefs) for side in sides]

    def pair_step(i, way):
        own = state[i]
        other = [exchanged(block, pair[0], pair[1]) for block, pair in zip(own, way)]
        own, other = after((own, other), done)
        return [butterfly(a, b, pair[2]) for a, b, pair in zip(own, other, way)]

    def back_step(i):
        pieces = [jnp.concatenate([side[e] for side in state[i]], axis=2) for e in range(4)]
        return pieces[:1] + [exchanged(pieces[d], "gz", d * stride) for d in range(1, 4)]

    steps = len(ways) + 1
    order = sorted((2 * i + step - (step > 0) * 0.5, i, step) for i in range(len(chunks)) for step in range(steps))
    back = [None] * len(chunks)
    for _, i, step in order:
        state[i] = mix_step(i) if step == 0 else pair_step(i, ways[step - 1])
        done = state[i]
        if step == steps - 1:
            back[i] = back_step(i)
    result = None
    for (start, _), pieces in zip(chunks, back):
        result = finish(pieces, right, left, result, start, planes)
    return result


def solution(mesh):
    in_specs = (P(None, None, "gy", "gz"),)
    out_specs = P(None, None, "gy", "gz")
    return jax.shard_map(shards, mesh=mesh, in_specs=in_specs, out_specs=out_specs, check_vma=False)
```

```python
import functools
import math

import jax
import jax.numpy as jnp
from jax import lax
from jax.experimental import pallas as pl
from jax.experimental.pallas import tpu as pltpu
from jax.sharding import PartitionSpec as P


GRANT = 16 * 2**20

F32 = jnp.float32
BF16 = jnp.bfloat16
SMEM = pl.BlockSpec(memory_space=pltpu.SMEM)
VMEM = pl.BlockSpec(memory_space=pltpu.VMEM)
ANY = pl.BlockSpec(memory_space=pl.ANY)


def exchanged(block, axis, mask):
    count = lax.axis_size(axis)
    return lax.ppermute(block, axis, [(i, i ^ mask) for i in range(count)])


def reversed_bits(index, bit_count):
    result = index * 0
    for place in range(bit_count):
        result = result + ((index >> place) & 1) * 2 ** (bit_count - 1 - place)
    return result


def unit(products, length):
    phase = -2.0 * math.pi * (products % length).astype(F32) / length
    return jnp.cos(phase), jnp.sin(phase)


def estimate(flops, count):
    return pl.CostEstimate(flops=flops, transcendentals=0, bytes_accessed=4 * count)


def dft_matrix(frequency, count, local, at):
    length = count * local
    to = jnp.arange(local, dtype=jnp.int32)
    cosine, sine = unit(at[:, None] * (frequency + count * to[None, :]), length)
    scale = 1.0 / math.sqrt(length)
    return cosine * scale, sine * scale


def split(values):
    high = lax.reduce_precision(values, 8, 7)
    return jnp.stack([high.astype(BF16), (values - high).astype(BF16)])


def right_matrix(frequency, count, local):
    cosine, sine = dft_matrix(frequency, count, local, jnp.arange(local, dtype=jnp.int32))
    return split(jnp.block([[cosine, sine], [-sine, cosine]]))


def left_matrix(frequency, count, local, part):
    at = jnp.arange(local, dtype=jnp.int32)
    quarter = local // 4
    at = (part ^ (at // quarter)) * quarter + at % quarter
    cosine, sine = dft_matrix(frequency, count, local, at)
    return split(jnp.block([[cosine.T, -sine.T], [sine.T, cosine.T]]))


def halves(values):
    high = values.astype(BF16)
    return high, (values - high.astype(F32)).astype(BF16)


def dot3(left, right):
    def single(a, b):
        return jnp.dot(a, b, preferred_element_type=F32)

    return single(left[0], right[0]) + (single(left[1], right[0]) + single(left[0], right[1]))


def along_last(real, imag, matrix_ref):
    local = real.shape[-1]
    mixed = dot3(halves(jnp.concatenate([real, imag], axis=1)), (matrix_ref[0], matrix_ref[1]))
    return mixed[:, :local], mixed[:, local:]


def along_first(real, imag, matrix_ref):
    local = real.shape[0]
    mixed = dot3((matrix_ref[0], matrix_ref[1]), halves(jnp.concatenate([real, imag], axis=0)))
    return mixed[:local], mixed[local:]


def after(value, done):
    return value if done is None else lax.optimization_barrier((value, done))[0]


def turned(values, cosine, sine):
    sign = jnp.array([-1.0, 1.0], F32).reshape(2, 1, 1, 1)
    return values * cosine + jnp.flip(values, -4) * (sign * sine)


def mixed(pieces, coefs):
    total = None
    for d, piece in enumerate(pieces):
        term = turned(piece[None], coefs[0, :, d].reshape(4, 1, 1, 1, 1), coefs[1, :, d].reshape(4, 1, 1, 1, 1))
        total = term if total is None else total + term
    return total


def butterfly(own, other, pair):
    flip, twist = pair
    both = own * flip + other
    return both if twist is None else turned(both, *twist)


def finish_kernel(start, right_ref, left_ref, e0_ref, e1_ref, e2_ref, e3_ref, *rest):
    out_ref, done, sems = rest[-3:]
    planes = e0_ref.shape[1]
    copies = []
    for plane in range(planes):
        refs = (e0_ref, e1_ref, e2_ref, e3_ref)
        whole = [jnp.concatenate([ref[part, plane] for ref in refs], axis=0) for part in range(2)]
        real, imag = along_last(whole[0], whole[1], right_ref)
        real, imag = along_first(real, imag, left_ref)
        done[plane, 0] = real
        done[plane, 1] = imag
        copies.append(pltpu.make_async_copy(done.at[plane], out_ref.at[:, start + plane], sems.at[plane]))
        copies[-1].start()
    for copy in copies:
        copy.wait()


def finish(pieces, right, left, out, start, total):
    _, planes, quarter, columns = pieces[0].shape
    rows = 4 * quarter
    in_specs = [VMEM] * 6
    args = [right, left, *pieces]
    aliases = {}
    if out is not None:
        in_specs.append(ANY)
        aliases = {len(args): 0}
        args.append(out)
    return pl.pallas_call(
        functools.partial(finish_kernel, start),
        in_specs=in_specs,
        out_specs=ANY,
        out_shape=jax.ShapeDtypeStruct((2, total, rows, columns), F32),
        scratch_shapes=[
            pltpu.VMEM((planes, 2, rows, columns), F32),
            pltpu.SemaphoreType.DMA((planes,)),
        ],
        input_output_aliases=aliases,
        compiler_params=pltpu.CompilerParams(vmem_limit_bytes=GRANT),
        cost_estimate=estimate(24 * planes * rows * columns * (rows + columns), 4 * planes * rows * columns),
        name="finish",
    )(*args)


def pair_of(axis, index, bit):
    upper = (index >> bit) & 1
    lower = index % 2**bit
    flip = (1 - 2 * upper).astype(F32)
    return axis, 2**bit, (flip, unit(lower * upper, 2 ** (bit + 1)) if bit else None)


def mix_coefs(part, rest, count):
    step = jnp.arange(4, dtype=jnp.int32)
    k = reversed_bits(part ^ step, 2)[:, None]
    d = (part ^ step)[None, :]
    return jnp.stack(unit(rest * k + (count // 4) * (d * k), count))


def chunks_of(planes):
    size = max(1, planes // 3)
    starts = list(range(0, planes, size))
    return [(at, min(size, planes - at)) for at in starts]


def order_of(sizes, steps):
    ready, at, free, order = [], 0.5, 0.0, []
    for i, size in enumerate(sizes):
        at += size
        ready.append((at, i, 0))
    while ready:
        ready.sort()
        now, i, step = ready.pop(0)
        order.append((i, step))
        if step < steps - 2:
            free = max(now + 0.1, free) + sizes[i] / 2
            ready.append((free, i, step + 1))
        elif step < steps - 1:
            ready.append((now + 0.1, i, step + 1))
    return order


def shards(velocity):
    _, planes, rows, columns = velocity.shape
    z_count = lax.axis_size("gz")
    y_count = lax.axis_size("gy")
    z_bits = z_count.bit_length() - 1
    y_bits = y_count.bit_length() - 1
    z_index = lax.axis_index("gz")
    y_index = lax.axis_index("gy")
    stride = z_count // 4
    part = z_index // stride
    quarter = rows // 4
    coefs = mix_coefs(part, z_index % stride, z_count)
    right = right_matrix(reversed_bits(z_index, z_bits), z_count, columns)
    left = left_matrix(reversed_bits(y_index, y_bits), y_count, rows, part)
    z_pairs = [pair_of("gz", z_index, bit) for bit in reversed(range(z_bits - 2))]
    y_pairs = [pair_of("gy", y_index, bit) for bit in reversed(range(y_bits))]
    ways = list(zip(z_pairs + y_pairs[:-1], y_pairs[:-1] + z_pairs))
    ways.append((y_pairs[-1], y_pairs[-1]))

    chunks = chunks_of(planes)
    quarters = velocity.reshape(2, planes, 4, quarter, columns)
    received = []
    for start, size in chunks:
        shape = (2, size, 1, quarter, columns)
        pieces = [lax.dynamic_slice(quarters, (0, start, part ^ d, 0, 0), shape)[:, :, 0] for d in range(4)]
        received.append(pieces[:1] + [exchanged(pieces[d], "gz", d * stride) for d in range(1, 4)])

    state = [None] * len(chunks)
    done = None

    def mix_step(i):
        cut = quarter // 2
        pieces = after(received[i], done)
        return [mixed([piece[:, :, at : at + cut] for piece in pieces], coefs) for at in (0, cut)]

    def pair_step(i, way):
        own = state[i]
        other = [exchanged(block, pair[0], pair[1]) for block, pair in zip(own, way)]
        own, other = after((own, other), done)
        return [butterfly(a, b, pair[2]) for a, b, pair in zip(own, other, way)]

    def back_step(i):
        pieces = [jnp.concatenate([side[e] for side in state[i]], axis=2) for e in range(4)]
        return pieces[:1] + [exchanged(pieces[d], "gz", d * stride) for d in range(1, 4)]

    steps = len(ways) + 1
    order = order_of([size / chunks[0][1] for _, size in chunks], steps)
    back = [None] * len(chunks)
    for i, step in order:
        state[i] = mix_step(i) if step == 0 else pair_step(i, ways[step - 1])
        done = state[i]
        if step == steps - 1:
            back[i] = back_step(i)
    result = None
    for (start, _), pieces in zip(chunks, back):
        result = finish(pieces, right, left, result, start, planes)
    return result


def solution(mesh):
    in_specs = (P(None, None, "gy", "gz"),)
    out_specs = P(None, None, "gy", "gz")
    return jax.shard_map(shards, mesh=mesh, in_specs=in_specs, out_specs=out_specs, check_vma=False)
```

```python
import functools
import math

import jax
import jax.numpy as jnp
import numpy as np
from jax import lax
from jax.experimental import pallas as pl
from jax.experimental.pallas import tpu as pltpu
from jax.sharding import PartitionSpec as P


GRANT = 16 * 2**20

F32 = jnp.float32
BF16 = jnp.bfloat16
SMEM = pl.BlockSpec(memory_space=pltpu.SMEM)
VMEM = pl.BlockSpec(memory_space=pltpu.VMEM)
ANY = pl.BlockSpec(memory_space=pl.ANY)


def exchanged(block, axis, mask):
    count = lax.axis_size(axis)
    return lax.ppermute(block, axis, [(i, i ^ mask) for i in range(count)])


def reversed_bits(index, bit_count):
    return sum(((index >> place) & 1) << (bit_count - 1 - place) for place in range(bit_count))


def unit(products, length):
    phase = -2.0 * math.pi * (products % length).astype(F32) / length
    return jnp.cos(phase), jnp.sin(phase)


def estimate(flops, count):
    return pl.CostEstimate(flops=flops, transcendentals=0, bytes_accessed=4 * count)


def dft_matrix(frequency, count, local, at):
    length = count * local
    to = jnp.arange(local, dtype=jnp.int32)
    cosine, sine = unit(at[:, None] * (frequency + count * to[None, :]), length)
    scale = 1.0 / math.sqrt(length)
    return cosine * scale, sine * scale


def split(values):
    high = lax.reduce_precision(values, 8, 7)
    return jnp.stack([high.astype(BF16), (values - high).astype(BF16)])


def right_matrix(frequency, count, local):
    cosine, sine = dft_matrix(frequency, count, local, jnp.arange(local, dtype=jnp.int32))
    return split(jnp.block([[cosine, sine], [-sine, cosine]]))


def left_matrix(frequency, count, local, part):
    at = jnp.arange(local, dtype=jnp.int32)
    quarter = local // 4
    at = (part ^ (at // quarter)) * quarter + at % quarter
    cosine, sine = dft_matrix(frequency, count, local, at)
    return split(jnp.block([[cosine.T, -sine.T], [sine.T, cosine.T]]))


def halves(values):
    high = values.astype(BF16)
    return high, (values - high.astype(F32)).astype(BF16)


def dot3(left, right):
    def single(a, b):
        return jnp.dot(a, b, preferred_element_type=F32)

    return single(left[0], right[0]) + (single(left[1], right[0]) + single(left[0], right[1]))


def along_last(real, imag, matrix_ref):
    local = real.shape[-1]
    mixed = dot3(halves(jnp.concatenate([real, imag], axis=1)), (matrix_ref[0], matrix_ref[1]))
    return mixed[:, :local], mixed[:, local:]


def along_first(real, imag, matrix_ref):
    local = real.shape[0]
    mixed = dot3((matrix_ref[0], matrix_ref[1]), halves(jnp.concatenate([real, imag], axis=0)))
    return mixed[:local], mixed[local:]


def after(value, done):
    return value if done is None else lax.optimization_barrier((value, done))[0]


def turned(values, cosine, sine):
    real, imag = values[:, :1], values[:, 1:]
    return jnp.concatenate([real * cosine - imag * sine, real * sine + imag * cosine], axis=1)


def butterfly(own, other, pair, bit):
    both = own * pair[0] + other
    return turned(both, pair[1], pair[2]) if bit else both


def per_rows(planes, rows, step, body):
    def one(at, carry):
        body(at // (rows // step), pl.multiple_of(at % (rows // step) * step, step))
        return carry

    lax.fori_loop(0, planes * (rows // step), one, 0, unroll=4)


def mix_kernel(coef_ref, *refs):
    pieces, outs = refs[:4], refs[4:]
    planes, half = outs[0].shape[2:4]
    for h, out_ref in enumerate(outs):

        def body(plane, at, h=h, out_ref=out_ref):
            rows = pl.ds(h * half + at, 8)
            values = [(ref[0, plane, rows, :], ref[1, plane, rows, :]) for ref in pieces]
            for e in range(4):
                real, imag = None, None
                for d in range(4):
                    c, s = coef_ref[4 * e + d], coef_ref[16 + 4 * e + d]
                    a, b = values[d]
                    re, im = a * c - b * s, a * s + b * c
                    real = re if real is None else real + re
                    imag = im if imag is None else imag + im
                out_ref[e, 0, plane, pl.ds(at, 8), :] = real
                out_ref[e, 1, plane, pl.ds(at, 8), :] = imag

        per_rows(planes, half, 8, body)


def mix(pieces, coefs):
    _, planes, quarter, columns = pieces[0].shape
    half = jax.ShapeDtypeStruct((4, 2, planes, quarter // 2, columns), F32)
    return pl.pallas_call(
        mix_kernel,
        in_specs=[SMEM] + [VMEM] * 4,
        out_specs=[VMEM] * 2,
        out_shape=[half] * 2,
        compiler_params=pltpu.CompilerParams(vmem_limit_bytes=GRANT),
        cost_estimate=estimate(128 * planes * quarter * columns, 16 * planes * quarter * columns),
        name="mix",
    )(coefs, *pieces)


def join_kernel(twist, coef_ref, *refs):
    sides, outs = (refs[0:2], refs[2:4]), refs[4:]
    groups, _, planes, half, _ = refs[0].shape
    flip = coef_ref[0]
    for h, (own_ref, other_ref) in enumerate(sides):

        def body(plane, at, h=h, own_ref=own_ref, other_ref=other_ref):
            rows, into = pl.ds(at, 8), pl.ds(h * half + at, 8)
            for e in range(groups):
                real, imag = [own_ref[e, p, plane, rows, :] * flip + other_ref[e, p, plane, rows, :] for p in range(2)]
                if twist:
                    real, imag = real * coef_ref[1] - imag * coef_ref[2], real * coef_ref[2] + imag * coef_ref[1]
                outs[e][0, plane, into, :] = real
                outs[e][1, plane, into, :] = imag

        per_rows(planes, half, 8, body)


def join(own, other, pair, bit):
    groups, _, planes, half, columns = own[0].shape
    piece = jax.ShapeDtypeStruct((2, planes, 2 * half, columns), F32)
    return pl.pallas_call(
        functools.partial(join_kernel, bit > 0),
        in_specs=[SMEM] + [VMEM] * 4,
        out_specs=[VMEM] * groups,
        out_shape=[piece] * groups,
        compiler_params=pltpu.CompilerParams(vmem_limit_bytes=GRANT),
        cost_estimate=estimate(10 * own[0].size, 6 * own[0].size),
        name="join",
    )(pair, own[0], other[0], own[1], other[1])


def finish_kernel(start, right_ref, left_ref, e0_ref, e1_ref, e2_ref, e3_ref, *rest):
    out_ref, done, sems = rest[-3:]
    planes = e0_ref.shape[1]
    copies = []
    for plane in range(planes):
        refs = (e0_ref, e1_ref, e2_ref, e3_ref)
        whole = [jnp.concatenate([ref[part, plane] for ref in refs], axis=0) for part in range(2)]
        real, imag = along_last(whole[0], whole[1], right_ref)
        real, imag = along_first(real, imag, left_ref)
        done[plane, 0] = real
        done[plane, 1] = imag
        copies.append(pltpu.make_async_copy(done.at[plane], out_ref.at[:, start + plane], sems.at[plane]))
        copies[-1].start()
    for copy in copies:
        copy.wait()


def finish(pieces, right, left, out, start, total):
    _, planes, quarter, columns = pieces[0].shape
    rows = 4 * quarter
    in_specs = [VMEM] * 6
    args = [right, left, *pieces]
    aliases = {}
    if out is not None:
        in_specs.append(ANY)
        aliases = {len(args): 0}
        args.append(out)
    return pl.pallas_call(
        functools.partial(finish_kernel, start),
        in_specs=in_specs,
        out_specs=ANY,
        out_shape=jax.ShapeDtypeStruct((2, total, rows, columns), F32),
        scratch_shapes=[
            pltpu.VMEM((planes, 2, rows, columns), F32),
            pltpu.SemaphoreType.DMA((planes,)),
        ],
        input_output_aliases=aliases,
        compiler_params=pltpu.CompilerParams(vmem_limit_bytes=GRANT),
        cost_estimate=estimate(24 * planes * rows * columns * (rows + columns), 4 * planes * rows * columns),
        name="finish",
    )(*args)


def host_unit(products, length):
    value = np.exp(-2j * np.pi * (np.asarray(products) % length) / length)
    return value.real, value.imag


def pair_table(count, bit):
    index = np.arange(count)
    upper = (index >> bit) & 1
    return np.stack([1 - 2 * upper, *host_unit((index % 2**bit) * upper, 2 ** (bit + 1))], axis=1)


def mix_table(count):
    index, step = np.arange(count), np.arange(4)
    part, rest = index // (count // 4), index % (count // 4)
    k = reversed_bits(part[:, None] ^ step, 2)[:, :, None]
    d = (part[:, None] ^ step)[:, None, :]
    cosine, sine = host_unit(rest[:, None, None] * k + (count // 4) * (d * k), count)
    return np.concatenate([cosine.reshape(count, 16), sine.reshape(count, 16)], axis=1)


def row_of(table, index):
    table = jnp.asarray(table, F32)
    row = lax.dynamic_slice(table, (index, jnp.uint32(0)), (1, table.shape[1]))
    return row.reshape(table.shape[1])


def chunks_of(planes):
    size = max(1, planes // 3)
    starts = list(range(0, planes, size))
    return [(at, min(size, planes - at)) for at in starts]


def order_of(chunks, steps):
    sizes = [size / chunks[0][1] for _, size in chunks]
    ready, at, free, order = [], 0.5, 0.0, []
    for i, size in enumerate(sizes):
        at += size
        ready.append((at, i, 0))
    while ready:
        ready.sort()
        now, i, step = ready.pop(0)
        order.append((i, step))
        if step < steps - 2:
            free = max(now + 0.1, free) + sizes[i] / 2
            ready.append((free, i, step + 1))
        elif step < steps - 1:
            ready.append((now + 0.1, i, step + 1))
    return order


def shards(velocity):
    _, planes, rows, columns = velocity.shape
    z_count = lax.axis_size("gz")
    y_count = lax.axis_size("gy")
    z_bits = z_count.bit_length() - 1
    y_bits = y_count.bit_length() - 1
    stride = z_count // 4
    quarter = rows // 4
    z_index = lax.axis_index("gz").astype(jnp.uint32)
    y_index = lax.axis_index("gy").astype(jnp.uint32)
    part = z_index >> (z_bits - 2)
    peers = [part ^ d for d in range(4)]
    shifts = [reversed_bits(z_index, z_bits), reversed_bits(y_index, y_bits)]
    velocity, z_index, y_index, part, peers, shifts = lax.optimization_barrier(
        (velocity, z_index, y_index, part, peers, shifts)
    )

    chunks = chunks_of(planes)
    quarters = velocity.reshape(2, planes, 4, quarter, columns)
    received = []
    zero = jnp.uint32(0)
    for start, size in chunks:
        shape = (2, size, 1, quarter, columns)
        at = jnp.uint32(start)
        pieces = [lax.dynamic_slice(quarters, (zero, at, peer, zero, zero), shape)[:, :, 0] for peer in peers]
        quarters = after(quarters, pieces)
        received.append(pieces[:1] + [exchanged(pieces[d], "gz", d * stride) for d in range(1, 4)])

    coefs = row_of(mix_table(z_count), z_index)
    right = right_matrix(shifts[0].astype(jnp.int32), z_count, columns)
    left = left_matrix(shifts[1].astype(jnp.int32), y_count, rows, part.astype(jnp.int32))
    z_pairs = [("gz", bit, row_of(pair_table(z_count, bit), z_index)) for bit in reversed(range(z_bits - 2))]
    y_pairs = [("gy", bit, row_of(pair_table(y_count, bit), y_index)) for bit in reversed(range(y_bits))]
    ways = list(zip(z_pairs + y_pairs[:-1], y_pairs[:-1] + z_pairs))
    ways.append((y_pairs[-1], y_pairs[-1]))

    state = [None] * len(chunks)
    done = None
    steps = len(ways) + 1
    back = [None] * len(chunks)
    for i, step in order_of(chunks, steps):
        if step == 0:
            pieces = after(received[i], done)
            state[i] = mix(pieces, coefs)
        else:
            way = ways[step - 1]
            other = [exchanged(block, axis, 2**bit) for block, (axis, bit, _) in zip(state[i], way)]
            own, other = after((state[i], other), done)
            if step == steps - 1:
                pieces = list(join(own, other, way[0][2], way[0][1]))
            else:
                pieces = [butterfly(a, b, pair, bit) for a, b, (_, bit, pair) in zip(own, other, way)]
            state[i] = pieces
            if step == steps - 1:
                back[i] = pieces[:1] + [exchanged(pieces[d], "gz", d * stride) for d in range(1, 4)]
        done = state[i]
    result = None
    for i, (start, _) in enumerate(chunks):
        result = finish(back[i], right, left, result, start, planes)
    return result


def solution(mesh):
    in_specs = (P(None, None, "gy", "gz"),)
    out_specs = P(None, None, "gy", "gz")
    return jax.shard_map(shards, mesh=mesh, in_specs=in_specs, out_specs=out_specs, check_vma=False)
```

```python
import functools
import math

import jax
import jax.numpy as jnp
import numpy as np
from jax import lax
from jax.experimental import pallas as pl
from jax.experimental.pallas import tpu as pltpu
from jax.sharding import PartitionSpec as P


GRANT = 16 * 2**20

F32 = jnp.float32
BF16 = jnp.bfloat16
SMEM = pl.BlockSpec(memory_space=pltpu.SMEM)
VMEM = pl.BlockSpec(memory_space=pltpu.VMEM)
ANY = pl.BlockSpec(memory_space=pl.ANY)


def exchanged(block, axis, mask):
    count = lax.axis_size(axis)
    return lax.ppermute(block, axis, [(i, i ^ mask) for i in range(count)])


def reversed_bits(index, bit_count):
    return sum(((index >> place) & 1) << (bit_count - 1 - place) for place in range(bit_count))


def unit(products, length):
    phase = -2.0 * math.pi * (products % length).astype(F32) / length
    return jnp.cos(phase), jnp.sin(phase)


def estimate(flops, count):
    return pl.CostEstimate(flops=flops, transcendentals=0, bytes_accessed=4 * count)


def dft_matrix(frequency, count, local, at):
    length = count * local
    to = jnp.arange(local, dtype=jnp.int32)
    cosine, sine = unit(at[:, None] * (frequency + count * to[None, :]), length)
    scale = 1.0 / math.sqrt(length)
    return cosine * scale, sine * scale


def split(values):
    high = lax.reduce_precision(values, 8, 7)
    return jnp.stack([high.astype(BF16), (values - high).astype(BF16)])


def right_matrix(frequency, count, local):
    cosine, sine = dft_matrix(frequency, count, local, jnp.arange(local, dtype=jnp.int32))
    return split(jnp.block([[cosine, sine], [-sine, cosine]]))


def left_matrix(frequency, count, local, part):
    at = jnp.arange(local, dtype=jnp.int32)
    quarter = local // 4
    at = (part ^ (at // quarter)) * quarter + at % quarter
    cosine, sine = dft_matrix(frequency, count, local, at)
    return split(jnp.block([[cosine.T, -sine.T], [sine.T, cosine.T]]))


def halves(values):
    high = values.astype(BF16)
    return high, (values - high.astype(F32)).astype(BF16)


def dot3(left, right):
    def single(a, b):
        return jnp.dot(a, b, preferred_element_type=F32)

    return single(left[0], right[0]) + (single(left[1], right[0]) + single(left[0], right[1]))


def along_last(real, imag, matrix_ref):
    local = real.shape[-1]
    mixed = dot3(halves(jnp.concatenate([real, imag], axis=1)), (matrix_ref[0], matrix_ref[1]))
    return mixed[:, :local], mixed[:, local:]


def along_first(real, imag, matrix_ref):
    local = real.shape[0]
    mixed = dot3((matrix_ref[0], matrix_ref[1]), halves(jnp.concatenate([real, imag], axis=0)))
    return mixed[:local], mixed[local:]


def after(value, done):
    return value if done is None else lax.optimization_barrier((value, done))[0]


def per_rows(planes, rows, step, body):
    def one(at, carry):
        body(at // (rows // step), pl.multiple_of(at % (rows // step) * step, step))
        return carry

    lax.fori_loop(0, planes * (rows // step), one, 0, unroll=4)


def mix_kernel(coef_ref, *refs):
    pieces, outs = refs[:4], refs[4:]
    planes, half = outs[0].shape[2:4]
    for h, out_ref in enumerate(outs):

        def body(plane, at, h=h, out_ref=out_ref):
            rows = pl.ds(h * half + at, 8)
            values = [(ref[0, plane, rows, :], ref[1, plane, rows, :]) for ref in pieces]
            for e in range(4):
                real, imag = None, None
                for d in range(4):
                    c, s = coef_ref[4 * e + d], coef_ref[16 + 4 * e + d]
                    a, b = values[d]
                    re, im = a * c - b * s, a * s + b * c
                    real = re if real is None else real + re
                    imag = im if imag is None else imag + im
                out_ref[e, 0, plane, pl.ds(at, 8), :] = real
                out_ref[e, 1, plane, pl.ds(at, 8), :] = imag

        per_rows(planes, half, 8, body)


def mix(pieces, coefs):
    _, planes, quarter, columns = pieces[0].shape
    half = jax.ShapeDtypeStruct((4, 2, planes, quarter // 2, columns), F32)
    return pl.pallas_call(
        mix_kernel,
        in_specs=[SMEM] + [VMEM] * 4,
        out_specs=[VMEM] * 2,
        out_shape=[half] * 2,
        compiler_params=pltpu.CompilerParams(vmem_limit_bytes=GRANT),
        cost_estimate=estimate(128 * planes * quarter * columns, 16 * planes * quarter * columns),
        name="mix",
    )(coefs, *pieces)


def butterfly_kernel(kinds, apart, *refs):
    sides, outs = refs[2:6], refs[6:]
    groups, _, planes, half, _ = sides[0].shape
    for h, (source, at_coef, twist) in enumerate(kinds):
        coef_ref, own_ref, other_ref = refs[source], sides[2 * h], sides[2 * h + 1]
        flip, c, s = [coef_ref[at_coef + i] for i in range(3)]

        def body(plane, at):
            rows = pl.ds(at, 8)
            for e in range(groups):
                real, imag = [own_ref[e, p, plane, rows, :] * flip + other_ref[e, p, plane, rows, :] for p in range(2)]
                if twist:
                    real, imag = real * c - imag * s, real * s + imag * c
                if apart:
                    into = pl.ds(h * half + at, 8)
                    outs[e][0, plane, into, :] = real
                    outs[e][1, plane, into, :] = imag
                else:
                    outs[h][e, 0, plane, rows, :] = real
                    outs[h][e, 1, plane, rows, :] = imag

        per_rows(planes, half, 8, body)


def butterfly(own, other, kinds, coefs, apart):
    groups, _, planes, half, columns = own[0].shape
    if apart:
        shapes = [jax.ShapeDtypeStruct((2, planes, 2 * half, columns), F32)] * groups
    else:
        shapes = [jax.ShapeDtypeStruct(own[0].shape, F32)] * 2
    return list(
        pl.pallas_call(
            functools.partial(butterfly_kernel, kinds, apart),
            in_specs=[SMEM] * 2 + [VMEM] * 4,
            out_specs=[VMEM] * len(shapes),
            out_shape=shapes,
            compiler_params=pltpu.CompilerParams(vmem_limit_bytes=GRANT),
            cost_estimate=estimate(10 * own[0].size, 6 * own[0].size),
            name="butterfly",
        )(*coefs, own[0], other[0], own[1], other[1])
    )


def finish_kernel(start, right_ref, left_ref, e0_ref, e1_ref, e2_ref, e3_ref, *rest):
    out_ref, done, sems = rest[-3:]
    planes = e0_ref.shape[1]
    copies = []
    for plane in range(planes):
        refs = (e0_ref, e1_ref, e2_ref, e3_ref)
        whole = [jnp.concatenate([ref[part, plane] for ref in refs], axis=0) for part in range(2)]
        real, imag = along_last(whole[0], whole[1], right_ref)
        real, imag = along_first(real, imag, left_ref)
        done[plane, 0] = real
        done[plane, 1] = imag
        copies.append(pltpu.make_async_copy(done.at[plane], out_ref.at[:, start + plane], sems.at[plane]))
        copies[-1].start()
    for copy in copies:
        copy.wait()


def finish(pieces, right, left, out, start, total):
    _, planes, quarter, columns = pieces[0].shape
    rows = 4 * quarter
    in_specs = [VMEM] * 6
    args = [right, left, *pieces]
    aliases = {}
    if out is not None:
        in_specs.append(ANY)
        aliases = {len(args): 0}
        args.append(out)
    return pl.pallas_call(
        functools.partial(finish_kernel, start),
        in_specs=in_specs,
        out_specs=ANY,
        out_shape=jax.ShapeDtypeStruct((2, total, rows, columns), F32),
        scratch_shapes=[
            pltpu.VMEM((planes, 2, rows, columns), F32),
            pltpu.SemaphoreType.DMA((planes,)),
        ],
        input_output_aliases=aliases,
        compiler_params=pltpu.CompilerParams(vmem_limit_bytes=GRANT),
        cost_estimate=estimate(24 * planes * rows * columns * (rows + columns), 4 * planes * rows * columns),
        name="finish",
    )(*args)


def host_unit(products, length):
    value = np.exp(-2j * np.pi * (np.asarray(products) % length) / length)
    return value.real, value.imag


def pair_table(count, bit):
    index = np.arange(count)
    upper = (index >> bit) & 1
    return np.stack([1 - 2 * upper, *host_unit((index % 2**bit) * upper, 2 ** (bit + 1))], axis=1)


def mix_table(count):
    index, step = np.arange(count), np.arange(4)
    part, rest = index // (count // 4), index % (count // 4)
    k = reversed_bits(part[:, None] ^ step, 2)[:, :, None]
    d = (part[:, None] ^ step)[:, None, :]
    cosine, sine = host_unit(rest[:, None, None] * k + (count // 4) * (d * k), count)
    return np.concatenate([cosine.reshape(count, 16), sine.reshape(count, 16)], axis=1)


def row_of(table, index):
    table = jnp.asarray(table, F32)
    row = lax.dynamic_slice(table, (index, jnp.uint32(0)), (1, table.shape[1]))
    return row.reshape(table.shape[1])


def chunks_of(planes):
    edge = max(1, planes // 6)
    middle = max(1, (planes - 2 * edge + 1) // 2)
    starts, chunks = 0, []
    for size in (edge, middle, planes - 2 * edge - middle, edge):
        size = min(size, planes - starts)
        if size > 0:
            chunks.append((starts, size))
            starts += size
    return chunks


def order_of(chunks, steps):
    ready, at, free, order = [], 0.5, 0.0, []
    for i, (_, size) in enumerate(chunks):
        at += size
        ready.append((at, i, 0))
    while ready:
        ready.sort()
        now, i, step = ready.pop(0)
        order.append((i, step))
        if step < steps - 2:
            free = max(now + 0.2, free) + chunks[i][1] / 2
            ready.append((free, i, step + 1))
        elif step < steps - 1:
            ready.append((now + 0.3, i, step + 1))
    return order


def shards(velocity):
    _, planes, rows, columns = velocity.shape
    z_count = lax.axis_size("gz")
    y_count = lax.axis_size("gy")
    z_bits = z_count.bit_length() - 1
    y_bits = y_count.bit_length() - 1
    stride = z_count // 4
    quarter = rows // 4
    z_index = lax.axis_index("gz").astype(jnp.uint32)
    y_index = lax.axis_index("gy").astype(jnp.uint32)
    part = z_index >> (z_bits - 2)
    peers = [part ^ d for d in range(4)]
    shifts = [reversed_bits(z_index, z_bits), reversed_bits(y_index, y_bits)]
    velocity, z_index, y_index, part, peers, shifts = lax.optimization_barrier(
        (velocity, z_index, y_index, part, peers, shifts)
    )

    chunks = chunks_of(planes)
    quarters = velocity.reshape(2, planes, 4, quarter, columns)
    received = []
    zero = jnp.uint32(0)
    for start, size in chunks:
        shape = (2, size, 1, quarter, columns)
        at = jnp.uint32(start)
        pieces = [lax.dynamic_slice(quarters, (zero, at, peer, zero, zero), shape)[:, :, 0] for peer in peers]
        quarters = after(quarters, pieces)
        received.append(pieces[:1] + [exchanged(pieces[d], "gz", d * stride) for d in range(1, 4)])

    z_steps, y_steps = list(reversed(range(z_bits - 2))), list(reversed(range(y_bits)))
    z_table = np.concatenate([mix_table(z_count)] + [pair_table(z_count, bit) for bit in z_steps], axis=1)
    y_table = np.concatenate([pair_table(y_count, bit) for bit in y_steps], axis=1)
    coefs = [row_of(z_table, z_index), row_of(y_table, y_index)]
    right = right_matrix(shifts[0].astype(jnp.int32), z_count, columns)
    left = left_matrix(shifts[1].astype(jnp.int32), y_count, rows, part.astype(jnp.int32))
    z_pairs = [("gz", bit, (0, 32 + 3 * i, bit > 0)) for i, bit in enumerate(z_steps)]
    y_pairs = [("gy", bit, (1, 3 * i, bit > 0)) for i, bit in enumerate(y_steps)]
    ways = list(zip(z_pairs + y_pairs[:-1], y_pairs[:-1] + z_pairs))
    ways.append((y_pairs[-1], y_pairs[-1]))

    state = [None] * len(chunks)
    done = None
    steps = len(ways) + 1
    back = [None] * len(chunks)
    for i, step in order_of(chunks, steps):
        if step == 0:
            pieces = after(received[i], done)
            state[i] = mix(pieces, coefs[0])
        else:
            way = ways[step - 1]
            other = [exchanged(block, axis, 2**bit) for block, (axis, bit, _) in zip(state[i], way)]
            own, other = after((state[i], other), done)
            pieces = butterfly(own, other, tuple(pair for _, _, pair in way), coefs, step == steps - 1)
            state[i] = pieces
            if step == steps - 1:
                back[i] = pieces[:1] + [exchanged(pieces[d], "gz", d * stride) for d in range(1, 4)]
        done = state[i]
    result = None
    for i, (start, _) in enumerate(chunks):
        result = finish(back[i], right, left, result, start, planes)
    return result


def solution(mesh):
    in_specs = (P(None, None, "gy", "gz"),)
    out_specs = P(None, None, "gy", "gz")
    return jax.shard_map(shards, mesh=mesh, in_specs=in_specs, out_specs=out_specs, check_vma=False)
```

```python
import functools
import math

import jax
import jax.numpy as jnp
import numpy as np
from jax import lax
from jax.experimental import pallas as pl
from jax.experimental.pallas import tpu as pltpu
from jax.sharding import PartitionSpec as P


GRANT = 16 * 2**20

F32 = jnp.float32
BF16 = jnp.bfloat16
SMEM = pl.BlockSpec(memory_space=pltpu.SMEM)
VMEM = pl.BlockSpec(memory_space=pltpu.VMEM)
ANY = pl.BlockSpec(memory_space=pl.ANY)


def exchanged(block, axis, mask):
    count = lax.axis_size(axis)
    return lax.ppermute(block, axis, [(i, i ^ mask) for i in range(count)])


def reversed_bits(index, bit_count):
    return sum(((index >> place) & 1) << (bit_count - 1 - place) for place in range(bit_count))


def unit(products, length):
    phase = -2.0 * math.pi * (products % length).astype(F32) / length
    return jnp.cos(phase), jnp.sin(phase)


def estimate(flops, count):
    return pl.CostEstimate(flops=flops, transcendentals=0, bytes_accessed=4 * count)


def dft_matrix(frequency, count, local, at):
    length = count * local
    to = jnp.arange(local, dtype=jnp.int32)
    cosine, sine = unit(at[:, None] * (frequency + count * to[None, :]), length)
    scale = 1.0 / math.sqrt(length)
    return cosine * scale, sine * scale


def split(values):
    high = lax.reduce_precision(values, 8, 7)
    return jnp.stack([high.astype(BF16), (values - high).astype(BF16)])


def right_matrix(frequency, count, local):
    cosine, sine = dft_matrix(frequency, count, local, jnp.arange(local, dtype=jnp.int32))
    return split(jnp.block([[cosine, sine], [-sine, cosine]]))


def left_matrix(frequency, count, local, part):
    at = jnp.arange(local, dtype=jnp.int32)
    quarter = local // 4
    at = (part ^ (at // quarter)) * quarter + at % quarter
    cosine, sine = dft_matrix(frequency, count, local, at)
    return split(jnp.block([[cosine.T, -sine.T], [sine.T, cosine.T]]))


def halves(values):
    high = values.astype(BF16)
    return high, (values - high.astype(F32)).astype(BF16)


def dot3(left, right):
    def single(a, b):
        return jnp.dot(a, b, preferred_element_type=F32)

    return single(left[0], right[0]) + (single(left[1], right[0]) + single(left[0], right[1]))


def along_last(real, imag, matrix_ref):
    local = real.shape[-1]
    mixed = dot3(halves(jnp.concatenate([real, imag], axis=1)), (matrix_ref[0], matrix_ref[1]))
    return mixed[:, :local], mixed[:, local:]


def along_first(real, imag, matrix_ref):
    local = real.shape[0]
    mixed = dot3((matrix_ref[0], matrix_ref[1]), halves(jnp.concatenate([real, imag], axis=0)))
    return mixed[:local], mixed[local:]


def after(value, done):
    return value if done is None else lax.optimization_barrier((value, done))[0]


def per_rows(planes, rows, step, body):
    def one(at, carry):
        body(at // (rows // step), pl.multiple_of(at % (rows // step) * step, step))
        return carry

    lax.fori_loop(0, planes * (rows // step), one, 0, unroll=4)


def mix_kernel(coef_ref, *refs):
    pieces, outs = refs[:4], refs[4:]
    planes, half = outs[0].shape[2:4]
    for h, out_ref in enumerate(outs):

        def body(plane, at, h=h, out_ref=out_ref):
            rows = pl.ds(h * half + at, 8)
            values = [(ref[0, plane, rows, :], ref[1, plane, rows, :]) for ref in pieces]
            for e in range(4):
                real, imag = None, None
                for d in range(4):
                    c, s = coef_ref[4 * e + d], coef_ref[16 + 4 * e + d]
                    a, b = values[d]
                    re, im = a * c - b * s, a * s + b * c
                    real = re if real is None else real + re
                    imag = im if imag is None else imag + im
                out_ref[e, 0, plane, pl.ds(at, 8), :] = real
                out_ref[e, 1, plane, pl.ds(at, 8), :] = imag

        per_rows(planes, half, 8, body)


def mix(pieces, coefs):
    _, planes, quarter, columns = pieces[0].shape
    half = jax.ShapeDtypeStruct((4, 2, planes, quarter // 2, columns), F32)
    return pl.pallas_call(
        mix_kernel,
        in_specs=[SMEM] + [VMEM] * 4,
        out_specs=[VMEM] * 2,
        out_shape=[half] * 2,
        compiler_params=pltpu.CompilerParams(vmem_limit_bytes=GRANT),
        cost_estimate=estimate(128 * planes * quarter * columns, 16 * planes * quarter * columns),
        name="mix",
    )(coefs, *pieces)


def butterfly_kernel(kinds, apart, *refs):
    sides, outs = refs[2:6], refs[6:]
    groups, _, planes, half, _ = sides[0].shape
    for h, (source, at_coef, twist) in enumerate(kinds):
        coef_ref, own_ref, other_ref = refs[source], sides[2 * h], sides[2 * h + 1]
        flip, c, s = [coef_ref[at_coef + i] for i in range(3)]

        def body(plane, at):
            rows = pl.ds(at, 8)
            for e in range(groups):
                real, imag = [own_ref[e, p, plane, rows, :] * flip + other_ref[e, p, plane, rows, :] for p in range(2)]
                if twist:
                    real, imag = real * c - imag * s, real * s + imag * c
                if apart:
                    into = pl.ds(h * half + at, 8)
                    outs[e][0, plane, into, :] = real
                    outs[e][1, plane, into, :] = imag
                else:
                    outs[h][e, 0, plane, rows, :] = real
                    outs[h][e, 1, plane, rows, :] = imag

        per_rows(planes, half, 8, body)


def butterfly(own, other, kinds, coefs, apart):
    groups, _, planes, half, columns = own[0].shape
    if apart:
        shapes = [jax.ShapeDtypeStruct((2, planes, 2 * half, columns), F32)] * groups
    else:
        shapes = [jax.ShapeDtypeStruct(own[0].shape, F32)] * 2
    return list(
        pl.pallas_call(
            functools.partial(butterfly_kernel, kinds, apart),
            in_specs=[SMEM] * 2 + [VMEM] * 4,
            out_specs=[VMEM] * len(shapes),
            out_shape=shapes,
            compiler_params=pltpu.CompilerParams(vmem_limit_bytes=GRANT),
            cost_estimate=estimate(10 * own[0].size, 6 * own[0].size),
            name="butterfly",
        )(*coefs, own[0], other[0], own[1], other[1])
    )


def finish_kernel(start, right_ref, left_ref, e0_ref, e1_ref, e2_ref, e3_ref, *rest):
    out_ref, done, sems = rest[-3:]
    planes = e0_ref.shape[1]
    copies = []
    for plane in range(planes):
        refs = (e0_ref, e1_ref, e2_ref, e3_ref)
        whole = [jnp.concatenate([ref[part, plane] for ref in refs], axis=0) for part in range(2)]
        real, imag = along_last(whole[0], whole[1], right_ref)
        real, imag = along_first(real, imag, left_ref)
        done[plane, 0] = real
        done[plane, 1] = imag
        copies.append(pltpu.make_async_copy(done.at[plane], out_ref.at[:, start + plane], sems.at[plane]))
        copies[-1].start()
    for copy in copies:
        copy.wait()


def finish(pieces, right, left, out, start, total):
    _, planes, quarter, columns = pieces[0].shape
    rows = 4 * quarter
    in_specs = [VMEM] * 6
    args = [right, left, *pieces]
    aliases = {}
    if out is not None:
        in_specs.append(ANY)
        aliases = {len(args): 0}
        args.append(out)
    return pl.pallas_call(
        functools.partial(finish_kernel, start),
        in_specs=in_specs,
        out_specs=ANY,
        out_shape=jax.ShapeDtypeStruct((2, total, rows, columns), F32),
        scratch_shapes=[
            pltpu.VMEM((planes, 2, rows, columns), F32),
            pltpu.SemaphoreType.DMA((planes,)),
        ],
        input_output_aliases=aliases,
        compiler_params=pltpu.CompilerParams(vmem_limit_bytes=GRANT),
        cost_estimate=estimate(24 * planes * rows * columns * (rows + columns), 4 * planes * rows * columns),
        name="finish",
    )(*args)


def host_unit(products, length):
    value = np.exp(-2j * np.pi * (np.asarray(products) % length) / length)
    return value.real, value.imag


def pair_table(count, bit):
    index = np.arange(count)
    upper = (index >> bit) & 1
    return np.stack([1 - 2 * upper, *host_unit((index % 2**bit) * upper, 2 ** (bit + 1))], axis=1)


def mix_table(count):
    index, step = np.arange(count), np.arange(4)
    part, rest = index // (count // 4), index % (count // 4)
    k = reversed_bits(part[:, None] ^ step, 2)[:, :, None]
    d = (part[:, None] ^ step)[:, None, :]
    cosine, sine = host_unit(rest[:, None, None] * k + (count // 4) * (d * k), count)
    return np.concatenate([cosine.reshape(count, 16), sine.reshape(count, 16)], axis=1)


def row_of(table, index):
    table = jnp.asarray(table, F32)
    row = lax.dynamic_slice(table, (index, jnp.uint32(0)), (1, table.shape[1]))
    return row.reshape(table.shape[1])


def chunks_of(planes):
    edge = max(1, planes // 6)
    middle = max(1, (planes - 2 * edge + 1) // 2)
    starts, chunks = 0, []
    for size in (edge, middle, planes - 2 * edge - middle, edge):
        size = min(size, planes - starts)
        if size > 0:
            chunks.append((starts, size))
            starts += size
    return chunks


def plan_of(chunks, steps):
    events, ready, arrived = [], [], 0.1
    for i, (_, size) in enumerate(chunks):
        events.append((arrived, "go", i, 0))
        arrived += size + 0.15
        ready.append((arrived, i, 0))
    free, last = 0.0, {}
    while ready:
        ready.sort()
        now, i, step = ready.pop(0)
        events.append((now, "node", i, step))
        if step < steps - 2:
            free = max(now + 0.25, free) + chunks[i][1] / 2
            ready.append((free, i, step + 1))
        elif step < steps - 1:
            ready.append((now + 0.3, i, step + 1))
        else:
            last[i] = now + 0.1
    for i, (_, size) in enumerate(chunks):
        arrived = max(arrived, last[i])
        events.append((arrived, "back", i, 0))
        arrived += size + 0.15
        events.append((arrived, "end", i, 0))
    return [event[1:] for event in sorted(events, key=lambda event: (round(event[0], 3), event[1] == "node"))]


def shards(velocity):
    _, planes, rows, columns = velocity.shape
    z_count = lax.axis_size("gz")
    y_count = lax.axis_size("gy")
    z_bits = z_count.bit_length() - 1
    y_bits = y_count.bit_length() - 1
    stride = z_count // 4
    quarter = rows // 4
    z_index = lax.axis_index("gz").astype(jnp.uint32)
    y_index = lax.axis_index("gy").astype(jnp.uint32)
    part = z_index >> (z_bits - 2)
    peers = [part ^ d for d in range(4)]
    shifts = [reversed_bits(z_index, z_bits), reversed_bits(y_index, y_bits)]
    velocity, z_index, y_index, part, peers, shifts = lax.optimization_barrier(
        (velocity, z_index, y_index, part, peers, shifts)
    )

    chunks = chunks_of(planes)
    quarters = velocity.reshape(2, planes, 4, quarter, columns)
    received = []
    zero = jnp.uint32(0)
    for start, size in chunks:
        shape = (2, size, 1, quarter, columns)
        at = jnp.uint32(start)
        pieces = [lax.dynamic_slice(quarters, (zero, at, peer, zero, zero), shape)[:, :, 0] for peer in peers]
        quarters = after(quarters, pieces)
        received.append(pieces[:1] + [exchanged(pieces[d], "gz", d * stride) for d in range(1, 4)])

    z_steps, y_steps = list(reversed(range(z_bits - 2))), list(reversed(range(y_bits)))
    z_table = np.concatenate([mix_table(z_count)] + [pair_table(z_count, bit) for bit in z_steps], axis=1)
    y_table = np.concatenate([pair_table(y_count, bit) for bit in y_steps], axis=1)
    coefs = [row_of(z_table, z_index), row_of(y_table, y_index)]
    right = right_matrix(shifts[0].astype(jnp.int32), z_count, columns)
    left = left_matrix(shifts[1].astype(jnp.int32), y_count, rows, part.astype(jnp.int32))
    z_pairs = [("gz", bit, (0, 32 + 3 * i, bit > 0)) for i, bit in enumerate(z_steps)]
    y_pairs = [("gy", bit, (1, 3 * i, bit > 0)) for i, bit in enumerate(y_steps)]
    ways = list(zip(z_pairs + y_pairs[:-1], y_pairs[:-1] + z_pairs))
    ways.append((y_pairs[-1], y_pairs[-1]))

    state = [None] * len(chunks)
    done = None
    steps = len(ways) + 1
    back = [None] * len(chunks)
    result = None
    for kind, i, step in plan_of(chunks, steps):
        if kind == "node" and step == 0:
            pieces = after(received[i], done)
            state[i] = mix(pieces, coefs[0])
        elif kind == "node":
            way = ways[step - 1]
            other = [exchanged(block, axis, 2**bit) for block, (axis, bit, _) in zip(state[i], way)]
            own, other = after((state[i], other), done)
            state[i] = butterfly(own, other, tuple(pair for _, _, pair in way), coefs, step == steps - 1)
            if step == steps - 1:
                back[i] = state[i][:1] + [exchanged(state[i][d], "gz", d * stride) for d in range(1, 4)]
        elif kind == "end":
            pieces = after(back[i], done)
            result = finish(pieces, right, left, result, chunks[i][0], planes)
        done = result if kind == "end" else state[i] if kind == "node" else done
    return result


def solution(mesh):
    in_specs = (P(None, None, "gy", "gz"),)
    out_specs = P(None, None, "gy", "gz")
    return jax.shard_map(shards, mesh=mesh, in_specs=in_specs, out_specs=out_specs, check_vma=False)
```

```python
import functools
import math

import jax
import jax.numpy as jnp
import numpy as np
from jax import lax
from jax.experimental import pallas as pl
from jax.experimental.pallas import tpu as pltpu
from jax.sharding import PartitionSpec as P


GRANT = 16 * 2**20

F32 = jnp.float32
BF16 = jnp.bfloat16
SMEM = pl.BlockSpec(memory_space=pltpu.SMEM)
VMEM = pl.BlockSpec(memory_space=pltpu.VMEM)
ANY = pl.BlockSpec(memory_space=pl.ANY)


def exchanged(block, axis, mask):
    count = lax.axis_size(axis)
    return lax.ppermute(block, axis, [(i, i ^ mask) for i in range(count)])


def reversed_bits(index, bit_count):
    return sum(((index >> place) & 1) << (bit_count - 1 - place) for place in range(bit_count))


def unit(products, length):
    phase = -2.0 * math.pi * (products % length).astype(F32) / length
    return jnp.cos(phase), jnp.sin(phase)


def estimate(flops, count):
    return pl.CostEstimate(flops=flops, transcendentals=0, bytes_accessed=4 * count)


def dft_matrix(frequency, count, local, at):
    length = count * local
    to = jnp.arange(local, dtype=jnp.int32)
    cosine, sine = unit(at[:, None] * (frequency + count * to[None, :]), length)
    scale = 1.0 / math.sqrt(length)
    return cosine * scale, sine * scale


def split(values):
    high = lax.reduce_precision(values, 8, 7)
    return jnp.stack([high.astype(BF16), (values - high).astype(BF16)])


def right_matrix(frequency, count, local):
    cosine, sine = dft_matrix(frequency, count, local, jnp.arange(local, dtype=jnp.int32))
    return split(jnp.block([[cosine, sine], [-sine, cosine]]))


def left_matrix(frequency, count, local, part):
    at = jnp.arange(local, dtype=jnp.int32)
    quarter = local // 4
    at = (part ^ (at // quarter)) * quarter + at % quarter
    cosine, sine = dft_matrix(frequency, count, local, at)
    return split(jnp.block([[cosine.T, -sine.T], [sine.T, cosine.T]]))


def halves(values):
    high = values.astype(BF16)
    return high, (values - high.astype(F32)).astype(BF16)


def dot3(left, right):
    def single(a, b):
        return jnp.dot(a, b, preferred_element_type=F32)

    return single(left[0], right[0]) + (single(left[1], right[0]) + single(left[0], right[1]))


def along_last(real, imag, matrix_ref):
    local = real.shape[-1]
    mixed = dot3(halves(jnp.concatenate([real, imag], axis=1)), (matrix_ref[0], matrix_ref[1]))
    return mixed[:, :local], mixed[:, local:]


def along_first(real, imag, matrix_ref):
    local = real.shape[0]
    mixed = dot3((matrix_ref[0], matrix_ref[1]), halves(jnp.concatenate([real, imag], axis=0)))
    return mixed[:local], mixed[local:]


def after(value, done):
    return value if done is None else lax.optimization_barrier((value, done))[0]


def per_rows(planes, rows, step, body):
    def one(at, carry):
        body(at // (rows // step), pl.multiple_of(at % (rows // step) * step, step))
        return carry

    lax.fori_loop(0, planes * (rows // step), one, 0, unroll=4)


def mix_kernel(coef_ref, *refs):
    pieces, outs = refs[:4], refs[4:]
    planes, half = outs[0].shape[2:4]
    for h, out_ref in enumerate(outs):

        def body(plane, at, h=h, out_ref=out_ref):
            rows = pl.ds(h * half + at, 8)
            values = [(ref[0, plane, rows, :], ref[1, plane, rows, :]) for ref in pieces]
            for e in range(4):
                real, imag = None, None
                for d in range(4):
                    c, s = coef_ref[4 * e + d], coef_ref[16 + 4 * e + d]
                    a, b = values[d]
                    re, im = a * c - b * s, a * s + b * c
                    real = re if real is None else real + re
                    imag = im if imag is None else imag + im
                out_ref[e, 0, plane, pl.ds(at, 8), :] = real
                out_ref[e, 1, plane, pl.ds(at, 8), :] = imag

        per_rows(planes, half, 8, body)


def mix(pieces, coefs):
    _, planes, quarter, columns = pieces[0].shape
    half = jax.ShapeDtypeStruct((4, 2, planes, quarter // 2, columns), F32)
    return pl.pallas_call(
        mix_kernel,
        in_specs=[SMEM] + [VMEM] * 4,
        out_specs=[VMEM] * 2,
        out_shape=[half] * 2,
        compiler_params=pltpu.CompilerParams(vmem_limit_bytes=GRANT),
        cost_estimate=estimate(128 * planes * quarter * columns, 16 * planes * quarter * columns),
        name="mix",
    )(coefs, *pieces)


def butterfly_kernel(kinds, apart, *refs):
    sides, outs = refs[2:6], refs[6:]
    groups, _, planes, half, _ = sides[0].shape
    for h, (source, at_coef, twist) in enumerate(kinds):
        coef_ref, own_ref, other_ref = refs[source], sides[2 * h], sides[2 * h + 1]
        flip, c, s = [coef_ref[at_coef + i] for i in range(3)]

        def body(plane, at):
            rows = pl.ds(at, 8)
            for e in range(groups):
                real, imag = [own_ref[e, p, plane, rows, :] * flip + other_ref[e, p, plane, rows, :] for p in range(2)]
                if twist:
                    real, imag = real * c - imag * s, real * s + imag * c
                if apart:
                    into = pl.ds(h * half + at, 8)
                    outs[e][0, plane, into, :] = real
                    outs[e][1, plane, into, :] = imag
                else:
                    outs[h][e, 0, plane, rows, :] = real
                    outs[h][e, 1, plane, rows, :] = imag

        per_rows(planes, half, 8, body)


def butterfly(own, other, kinds, coefs, apart):
    groups, _, planes, half, columns = own[0].shape
    if apart:
        shapes = [jax.ShapeDtypeStruct((2, planes, 2 * half, columns), F32)] * groups
    else:
        shapes = [jax.ShapeDtypeStruct(own[0].shape, F32)] * 2
    return list(
        pl.pallas_call(
            functools.partial(butterfly_kernel, kinds, apart),
            in_specs=[SMEM] * 2 + [VMEM] * 4,
            out_specs=[VMEM] * len(shapes),
            out_shape=shapes,
            compiler_params=pltpu.CompilerParams(vmem_limit_bytes=GRANT),
            cost_estimate=estimate(10 * own[0].size, 6 * own[0].size),
            name="butterfly",
        )(*coefs, own[0], other[0], own[1], other[1])
    )


def finish_kernel(start, right_ref, left_ref, e0_ref, e1_ref, e2_ref, e3_ref, *rest):
    out_ref, done, sems = rest[-3:]
    planes = e0_ref.shape[1]
    copies = []
    for plane in range(planes):
        refs = (e0_ref, e1_ref, e2_ref, e3_ref)
        whole = [jnp.concatenate([ref[part, plane] for ref in refs], axis=0) for part in range(2)]
        real, imag = along_last(whole[0], whole[1], right_ref)
        real, imag = along_first(real, imag, left_ref)
        done[plane, 0] = real
        done[plane, 1] = imag
        copies.append(pltpu.make_async_copy(done.at[plane], out_ref.at[:, start + plane], sems.at[plane]))
        copies[-1].start()
    for copy in copies:
        copy.wait()


def finish(pieces, right, left, out, start, total):
    _, planes, quarter, columns = pieces[0].shape
    rows = 4 * quarter
    in_specs = [VMEM] * 6
    args = [right, left, *pieces]
    aliases = {}
    if out is not None:
        in_specs.append(ANY)
        aliases = {len(args): 0}
        args.append(out)
    return pl.pallas_call(
        functools.partial(finish_kernel, start),
        in_specs=in_specs,
        out_specs=ANY,
        out_shape=jax.ShapeDtypeStruct((2, total, rows, columns), F32),
        scratch_shapes=[
            pltpu.VMEM((planes, 2, rows, columns), F32),
            pltpu.SemaphoreType.DMA((planes,)),
        ],
        input_output_aliases=aliases,
        compiler_params=pltpu.CompilerParams(vmem_limit_bytes=GRANT),
        cost_estimate=estimate(24 * planes * rows * columns * (rows + columns), 4 * planes * rows * columns),
        name="finish",
    )(*args)


def host_unit(products, length):
    value = np.exp(-2j * np.pi * (np.asarray(products) % length) / length)
    return value.real, value.imag


def pair_table(count, bit):
    index = np.arange(count)
    upper = (index >> bit) & 1
    return np.stack([1 - 2 * upper, *host_unit((index % 2**bit) * upper, 2 ** (bit + 1))], axis=1)


def mix_table(count):
    index, step = np.arange(count), np.arange(4)
    part, rest = index // (count // 4), index % (count // 4)
    k = reversed_bits(part[:, None] ^ step, 2)[:, :, None]
    d = (part[:, None] ^ step)[:, None, :]
    cosine, sine = host_unit(rest[:, None, None] * k + (count // 4) * (d * k), count)
    return np.concatenate([cosine.reshape(count, 16), sine.reshape(count, 16)], axis=1)


def row_of(table, index):
    table = jnp.asarray(table, F32)
    row = lax.dynamic_slice(table, (index, jnp.uint32(0)), (1, table.shape[1]))
    return row.reshape(table.shape[1])


def chunks_of(planes):
    edge = max(1, planes // 6)
    middle = max(1, (planes - 2 * edge + 1) // 2)
    starts, chunks = 0, []
    for size in (edge, middle, planes - 2 * edge - middle, edge):
        size = min(size, planes - starts)
        if size > 0:
            chunks.append((starts, size))
            starts += size
    return chunks


def plan_of(chunks, steps):
    sizes = [size for _, size in chunks]
    count = len(sizes)
    arrive = [0.1 + sum(sizes[: i + 1]) + 0.1 * i for i in range(count)]
    end = arrive[-1] + 0.1 + sizes[0]
    events = [(arrive[i - 1] - 0.35 if i > 1 else 0.1 * i, "go", i, 0) for i in range(count)]
    early = arrive[-2] + 0.15 if count > 1 else 0.0
    if count > 1:
        arrive[0] += 0.5 * min(sizes[0], sizes[1])
        arrive[-1] += 0.7 * sizes[0]
    ready, free, last = [(at, i, 0) for i, at in enumerate(arrive)], 0.0, {}
    while ready:
        ready.sort()
        now, i, step = ready.pop(0)
        events.append((now, "node", i, step))
        if step < steps - 2:
            free = max(now + 0.25, free) + sizes[i] / 2
            ready.append((free, i, step + 1))
        elif step < steps - 1:
            ready.append((now + 0.3, i, step + 1))
        else:
            last[i] = now + 0.1
    early = max(early, last[0])
    events.append((early, "back", 0, 0))
    end = max(end, early + sizes[0])
    events.append((end, "end", 0, 0))
    for i in range(1, count):
        end = max(end, last[i])
        events.append((end - 0.35, "back", i, 0))
        end += sizes[i] + 0.1
        events.append((end, "end", i, 0))
    return [event[1:] for event in sorted(events)]


def shards(velocity):
    _, planes, rows, columns = velocity.shape
    z_count = lax.axis_size("gz")
    y_count = lax.axis_size("gy")
    z_bits = z_count.bit_length() - 1
    y_bits = y_count.bit_length() - 1
    stride = z_count // 4
    quarter = rows // 4
    z_index = lax.axis_index("gz").astype(jnp.uint32)
    y_index = lax.axis_index("gy").astype(jnp.uint32)
    part = z_index >> (z_bits - 2)
    peers = [part ^ d for d in range(4)]
    shifts = [reversed_bits(z_index, z_bits), reversed_bits(y_index, y_bits)]
    velocity, z_index, y_index, part, peers, shifts = lax.optimization_barrier(
        (velocity, z_index, y_index, part, peers, shifts)
    )

    chunks = chunks_of(planes)
    quarters = velocity.reshape(2, planes, 4, quarter, columns)
    received = []
    zero = jnp.uint32(0)
    for start, size in chunks:
        shape = (2, size, 1, quarter, columns)
        at = jnp.uint32(start)
        pieces = [lax.dynamic_slice(quarters, (zero, at, peer, zero, zero), shape)[:, :, 0] for peer in peers]
        quarters = after(quarters, pieces)
        received.append(pieces[:1] + [exchanged(pieces[d], "gz", d * stride) for d in range(1, 4)])

    z_steps, y_steps = list(reversed(range(z_bits - 2))), list(reversed(range(y_bits)))
    z_table = np.concatenate([mix_table(z_count)] + [pair_table(z_count, bit) for bit in z_steps], axis=1)
    y_table = np.concatenate([pair_table(y_count, bit) for bit in y_steps], axis=1)
    coefs = [row_of(z_table, z_index), row_of(y_table, y_index)]
    right = right_matrix(shifts[0].astype(jnp.int32), z_count, columns)
    left = left_matrix(shifts[1].astype(jnp.int32), y_count, rows, part.astype(jnp.int32))
    z_pairs = [("gz", bit, (0, 32 + 3 * i, bit > 0)) for i, bit in enumerate(z_steps)]
    y_pairs = [("gy", bit, (1, 3 * i, bit > 0)) for i, bit in enumerate(y_steps)]
    ways = list(zip(z_pairs + y_pairs[:-1], y_pairs[:-1] + z_pairs))
    ways.append((y_pairs[-1], y_pairs[-1]))

    state = [None] * len(chunks)
    done = None
    steps = len(ways) + 1
    back = [None] * len(chunks)
    result = None
    for kind, i, step in plan_of(chunks, steps):
        if kind == "node" and step == 0:
            pieces = after(received[i], done)
            state[i] = mix(pieces, coefs[0])
        elif kind == "node":
            way = ways[step - 1]
            other = [exchanged(block, axis, 2**bit) for block, (axis, bit, _) in zip(state[i], way)]
            own, other = after((state[i], other), done)
            state[i] = butterfly(own, other, tuple(pair for _, _, pair in way), coefs, step == steps - 1)
            if step == steps - 1:
                back[i] = state[i][:1] + [exchanged(state[i][d], "gz", d * stride) for d in range(1, 4)]
        elif kind == "end":
            pieces = after(back[i], done)
            result = finish(pieces, right, left, result, chunks[i][0], planes)
        done = result if kind == "end" else state[i] if kind == "node" else done
    return result


def solution(mesh):
    in_specs = (P(None, None, "gy", "gz"),)
    out_specs = P(None, None, "gy", "gz")
    return jax.shard_map(shards, mesh=mesh, in_specs=in_specs, out_specs=out_specs, check_vma=False)
```

```python
import functools
import math

import jax
import jax.numpy as jnp
import numpy as np
from jax import lax
from jax.experimental import pallas as pl
from jax.experimental.pallas import tpu as pltpu
from jax.sharding import PartitionSpec as P


GRANT = 16 * 2**20

F32 = jnp.float32
BF16 = jnp.bfloat16
SMEM = pl.BlockSpec(memory_space=pltpu.SMEM)
VMEM = pl.BlockSpec(memory_space=pltpu.VMEM)
ANY = pl.BlockSpec(memory_space=pl.ANY)


def exchanged(block, axis, mask):
    count = lax.axis_size(axis)
    return lax.ppermute(block, axis, [(i, i ^ mask) for i in range(count)])


def reversed_bits(index, bit_count):
    return sum(((index >> place) & 1) << (bit_count - 1 - place) for place in range(bit_count))


def unit(products, length):
    phase = -2.0 * math.pi * (products % length).astype(F32) / length
    return jnp.cos(phase), jnp.sin(phase)


def estimate(flops, count):
    return pl.CostEstimate(flops=flops, transcendentals=0, bytes_accessed=4 * count)


def dft_matrix(frequency, count, local, at):
    length = count * local
    to = jnp.arange(local, dtype=jnp.int32)
    cosine, sine = unit(at[:, None] * (frequency + count * to[None, :]), length)
    scale = 1.0 / math.sqrt(length)
    return cosine * scale, sine * scale


def split(values):
    high = lax.reduce_precision(values, 8, 7)
    return jnp.stack([high.astype(BF16), (values - high).astype(BF16)])


def right_matrix(frequency, count, local):
    cosine, sine = dft_matrix(frequency, count, local, jnp.arange(local, dtype=jnp.int32))
    return split(jnp.block([[cosine, sine], [-sine, cosine]]))


def left_matrix(frequency, count, local, part):
    at = jnp.arange(local, dtype=jnp.int32)
    quarter = local // 4
    at = (part ^ (at // quarter)) * quarter + at % quarter
    cosine, sine = dft_matrix(frequency, count, local, at)
    return split(jnp.block([[cosine.T, -sine.T], [sine.T, cosine.T]]))


def halves(values):
    high = values.astype(BF16)
    return high, (values - high.astype(F32)).astype(BF16)


def dot3(left, right):
    def single(a, b):
        return jnp.dot(a, b, preferred_element_type=F32)

    return single(left[0], right[0]) + (single(left[1], right[0]) + single(left[0], right[1]))


def along_last(real, imag, matrix_ref):
    local = real.shape[-1]
    mixed = dot3(halves(jnp.concatenate([real, imag], axis=1)), (matrix_ref[0], matrix_ref[1]))
    return mixed[:, :local], mixed[:, local:]


def along_first(real, imag, matrix_ref):
    local = real.shape[0]
    mixed = dot3((matrix_ref[0], matrix_ref[1]), halves(jnp.concatenate([real, imag], axis=0)))
    return mixed[:local], mixed[local:]


def after(value, done):
    return value if done is None else lax.optimization_barrier((value, done))[0]


def per_rows(planes, rows, step, body):
    def one(at, carry):
        body(at // (rows // step), pl.multiple_of(at % (rows // step) * step, step))
        return carry

    lax.fori_loop(0, planes * (rows // step), one, 0, unroll=4)


def mix_kernel(coef_ref, *refs):
    pieces, outs = refs[:4], refs[4:]
    planes, half = outs[0].shape[2:4]
    for h, out_ref in enumerate(outs):

        def body(plane, at, h=h, out_ref=out_ref):
            rows = pl.ds(h * half + at, 8)
            values = [(ref[0, plane, rows, :], ref[1, plane, rows, :]) for ref in pieces]
            for e in range(4):
                real, imag = None, None
                for d in range(4):
                    c, s = coef_ref[4 * e + d], coef_ref[16 + 4 * e + d]
                    a, b = values[d]
                    re, im = a * c - b * s, a * s + b * c
                    real = re if real is None else real + re
                    imag = im if imag is None else imag + im
                out_ref[e, 0, plane, pl.ds(at, 8), :] = real
                out_ref[e, 1, plane, pl.ds(at, 8), :] = imag

        per_rows(planes, half, 8, body)


def mix(pieces, coefs):
    _, planes, quarter, columns = pieces[0].shape
    half = jax.ShapeDtypeStruct((4, 2, planes, quarter // 2, columns), F32)
    return pl.pallas_call(
        mix_kernel,
        in_specs=[SMEM] + [VMEM] * 4,
        out_specs=[VMEM] * 2,
        out_shape=[half] * 2,
        compiler_params=pltpu.CompilerParams(vmem_limit_bytes=GRANT),
        cost_estimate=estimate(128 * planes * quarter * columns, 16 * planes * quarter * columns),
        name="mix",
    )(coefs, *pieces)


def butterfly_kernel(kinds, apart, *refs):
    sides, outs = refs[2:6], refs[6:]
    groups, _, planes, half, _ = sides[0].shape
    for h, (source, at_coef, twist) in enumerate(kinds):
        coef_ref, own_ref, other_ref = refs[source], sides[2 * h], sides[2 * h + 1]
        flip, c, s = [coef_ref[at_coef + i] for i in range(3)]

        def body(plane, at):
            rows = pl.ds(at, 8)
            for e in range(groups):
                real, imag = [own_ref[e, p, plane, rows, :] * flip + other_ref[e, p, plane, rows, :] for p in range(2)]
                if twist:
                    real, imag = real * c - imag * s, real * s + imag * c
                if apart:
                    into = pl.ds(h * half + at, 8)
                    outs[e][0, plane, into, :] = real
                    outs[e][1, plane, into, :] = imag
                else:
                    outs[h][e, 0, plane, rows, :] = real
                    outs[h][e, 1, plane, rows, :] = imag

        per_rows(planes, half, 8, body)


def butterfly(own, other, kinds, coefs, apart):
    groups, _, planes, half, columns = own[0].shape
    if apart:
        shapes = [jax.ShapeDtypeStruct((2, planes, 2 * half, columns), F32)] * groups
    else:
        shapes = [jax.ShapeDtypeStruct(own[0].shape, F32)] * 2
    return list(
        pl.pallas_call(
            functools.partial(butterfly_kernel, kinds, apart),
            in_specs=[SMEM] * 2 + [VMEM] * 4,
            out_specs=[VMEM] * len(shapes),
            out_shape=shapes,
            compiler_params=pltpu.CompilerParams(vmem_limit_bytes=GRANT),
            cost_estimate=estimate(10 * own[0].size, 6 * own[0].size),
            name="butterfly",
        )(*coefs, own[0], other[0], own[1], other[1])
    )


def finish_kernel(start, right_ref, left_ref, e0_ref, e1_ref, e2_ref, e3_ref, *rest):
    out_ref, done, sems = rest[-3:]
    planes = e0_ref.shape[1]
    copies = []
    for plane in range(planes):
        refs = (e0_ref, e1_ref, e2_ref, e3_ref)
        whole = [jnp.concatenate([ref[part, plane] for ref in refs], axis=0) for part in range(2)]
        real, imag = along_last(whole[0], whole[1], right_ref)
        real, imag = along_first(real, imag, left_ref)
        done[plane, 0] = real
        done[plane, 1] = imag
        copies.append(pltpu.make_async_copy(done.at[plane], out_ref.at[:, start + plane], sems.at[plane]))
        copies[-1].start()
    for copy in copies:
        copy.wait()


def finish(pieces, right, left, out, start, total):
    _, planes, quarter, columns = pieces[0].shape
    rows = 4 * quarter
    in_specs = [VMEM] * 6
    args = [right, left, *pieces]
    aliases = {}
    if out is not None:
        in_specs.append(ANY)
        aliases = {len(args): 0}
        args.append(out)
    return pl.pallas_call(
        functools.partial(finish_kernel, start),
        in_specs=in_specs,
        out_specs=ANY,
        out_shape=jax.ShapeDtypeStruct((2, total, rows, columns), F32),
        scratch_shapes=[
            pltpu.VMEM((planes, 2, rows, columns), F32),
            pltpu.SemaphoreType.DMA((planes,)),
        ],
        input_output_aliases=aliases,
        compiler_params=pltpu.CompilerParams(vmem_limit_bytes=GRANT),
        cost_estimate=estimate(24 * planes * rows * columns * (rows + columns), 4 * planes * rows * columns),
        name="finish",
    )(*args)


def host_unit(products, length):
    value = np.exp(-2j * np.pi * (np.asarray(products) % length) / length)
    return value.real, value.imag


def pair_table(count, bit):
    index = np.arange(count)
    upper = (index >> bit) & 1
    return np.stack([1 - 2 * upper, *host_unit((index % 2**bit) * upper, 2 ** (bit + 1))], axis=1)


def mix_table(count):
    index, step = np.arange(count), np.arange(4)
    part, rest = index // (count // 4), index % (count // 4)
    k = reversed_bits(part[:, None] ^ step, 2)[:, :, None]
    d = (part[:, None] ^ step)[:, None, :]
    cosine, sine = host_unit(rest[:, None, None] * k + (count // 4) * (d * k), count)
    return np.concatenate([cosine.reshape(count, 16), sine.reshape(count, 16)], axis=1)


def row_of(table, index):
    table = jnp.asarray(table, F32)
    row = lax.dynamic_slice(table, (index, jnp.uint32(0)), (1, table.shape[1]))
    return row.reshape(table.shape[1])


def chunks_of(planes):
    size = max(1, -(-planes // 3))
    return [(at, min(size, planes - at)) for at in range(0, planes, size)]


def plan_of(chunks, steps):
    events, ready, arrived = [], [], 0.1
    for i, (_, size) in enumerate(chunks):
        events.append((arrived - 0.35, "go", i, 0))
        arrived += size + 0.1
        ready.append((arrived, i, 0))
    free, last = 0.0, {}
    while ready:
        ready.sort()
        now, i, step = ready.pop(0)
        events.append((now, "node", i, step))
        if step < steps - 2:
            free = max(now + 0.25, free) + chunks[i][1] / 2
            ready.append((free, i, step + 1))
        elif step < steps - 1:
            ready.append((now + 0.3, i, step + 1))
        else:
            last[i] = now + 0.1
    for i, (_, size) in enumerate(chunks):
        arrived = max(arrived, last[i])
        events.append((arrived - 0.35, "back", i, 0))
        arrived += size + 0.1
        events.append((arrived, "end", i, 0))
    return [event[1:] for event in sorted(events)]


def shards(velocity):
    _, planes, rows, columns = velocity.shape
    z_count = lax.axis_size("gz")
    y_count = lax.axis_size("gy")
    z_bits = z_count.bit_length() - 1
    y_bits = y_count.bit_length() - 1
    stride = z_count // 4
    quarter = rows // 4
    z_index = lax.axis_index("gz").astype(jnp.uint32)
    y_index = lax.axis_index("gy").astype(jnp.uint32)
    part = z_index >> (z_bits - 2)
    peers = [part ^ d for d in range(4)]
    shifts = [reversed_bits(z_index, z_bits), reversed_bits(y_index, y_bits)]
    velocity, z_index, y_index, part, peers, shifts = lax.optimization_barrier(
        (velocity, z_index, y_index, part, peers, shifts)
    )

    chunks = chunks_of(planes)
    quarters = velocity.reshape(2, planes, 4, quarter, columns)
    received = []
    zero = jnp.uint32(0)
    for start, size in chunks:
        shape = (2, size, 1, quarter, columns)
        at = jnp.uint32(start)
        pieces = [lax.dynamic_slice(quarters, (zero, at, peer, zero, zero), shape)[:, :, 0] for peer in peers]
        quarters = after(quarters, pieces)
        received.append(pieces[:1] + [exchanged(pieces[d], "gz", d * stride) for d in range(1, 4)])

    z_steps, y_steps = list(reversed(range(z_bits - 2))), list(reversed(range(y_bits)))
    z_table = np.concatenate([mix_table(z_count)] + [pair_table(z_count, bit) for bit in z_steps], axis=1)
    y_table = np.concatenate([pair_table(y_count, bit) for bit in y_steps], axis=1)
    coefs = [row_of(z_table, z_index), row_of(y_table, y_index)]
    right = right_matrix(shifts[0].astype(jnp.int32), z_count, columns)
    left = left_matrix(shifts[1].astype(jnp.int32), y_count, rows, part.astype(jnp.int32))
    z_pairs = [("gz", bit, (0, 32 + 3 * i, bit > 0)) for i, bit in enumerate(z_steps)]
    y_pairs = [("gy", bit, (1, 3 * i, bit > 0)) for i, bit in enumerate(y_steps)]
    ways = list(zip(z_pairs + y_pairs[:-1], y_pairs[:-1] + z_pairs))
    ways.append((y_pairs[-1], y_pairs[-1]))

    state = [None] * len(chunks)
    done = None
    steps = len(ways) + 1
    back = [None] * len(chunks)
    result = None
    for kind, i, step in plan_of(chunks, steps):
        if kind == "node" and step == 0:
            pieces = after(received[i], done)
            state[i] = mix(pieces, coefs[0])
        elif kind == "node":
            way = ways[step - 1]
            other = [exchanged(block, axis, 2**bit) for block, (axis, bit, _) in zip(state[i], way)]
            own, other = after((state[i], other), done)
            state[i] = butterfly(own, other, tuple(pair for _, _, pair in way), coefs, step == steps - 1)
            if step == steps - 1:
                back[i] = state[i][:1] + [exchanged(state[i][d], "gz", d * stride) for d in range(1, 4)]
        elif kind == "end":
            pieces = after(back[i], done)
            result = finish(pieces, right, left, result, chunks[i][0], planes)
        done = result if kind == "end" else state[i] if kind == "node" else done
    return result


def solution(mesh):
    in_specs = (P(None, None, "gy", "gz"),)
    out_specs = P(None, None, "gy", "gz")
    return jax.shard_map(shards, mesh=mesh, in_specs=in_specs, out_specs=out_specs, check_vma=False)
```

```python
import functools
import math

import jax
import jax.numpy as jnp
import numpy as np
from jax import lax
from jax.experimental import pallas as pl
from jax.experimental.pallas import tpu as pltpu
from jax.sharding import PartitionSpec as P


GRANT = 16 * 2**20
LANES = (3, 2, 1)

F32 = jnp.float32
BF16 = jnp.bfloat16
SMEM = pl.BlockSpec(memory_space=pltpu.SMEM)
VMEM = pl.BlockSpec(memory_space=pltpu.VMEM)
ANY = pl.BlockSpec(memory_space=pl.ANY)


def exchanged(block, axis, mask):
    count = lax.axis_size(axis)
    return lax.ppermute(block, axis, [(i, i ^ mask) for i in range(count)])


def reversed_bits(index, bit_count):
    return sum(((index >> place) & 1) << (bit_count - 1 - place) for place in range(bit_count))


def unit(products, length):
    phase = -2.0 * math.pi * (products % length).astype(F32) / length
    return jnp.cos(phase), jnp.sin(phase)


def estimate(flops, count):
    return pl.CostEstimate(flops=flops, transcendentals=0, bytes_accessed=4 * count)


def dft_table(inputs, outputs, count, local, frequency):
    length = count * local
    turn = (inputs[1] - outputs[1]) * (length // 4)
    values = unit(inputs[0] * (frequency + count * outputs[0]) - turn, length)[0] * (1.0 / math.sqrt(length))
    high = lax.reduce_precision(values, 8, 7)
    return high.astype(BF16), (values - high).astype(BF16)


def right_tables(frequency, count, local):
    at = jnp.arange(2 * local, dtype=jnp.int32)
    at = at % local, at // local
    return dft_table([x[:, None] for x in at], [x[None, :] for x in at], count, local, frequency)


def left_tables(frequency, count, local, part):
    at = jnp.arange(2 * local, dtype=jnp.int32)
    quarter = local // 4
    row = (part ^ (at // (2 * quarter))) * quarter + at % quarter
    inputs = row[None, :], (at // quarter % 2)[None, :]
    return dft_table(inputs, [x[:, None] for x in (at % local, at // local)], count, local, frequency)


def halves(values):
    high = values.astype(BF16)
    return high, (values - high.astype(F32)).astype(BF16)


def dot3(left, right):
    def single(a, b):
        return jnp.dot(a, b, preferred_element_type=F32)

    return single(left[0], right[0]) + (single(left[1], right[0]) + single(left[0], right[1]))


def after(value, done):
    return value if done is None else lax.optimization_barrier((value, done))[0]


def per_rows(planes, rows, step, body):
    def one(at, carry):
        body(at // (rows // step), pl.multiple_of(at % (rows // step) * step, step))
        return carry

    lax.fori_loop(0, planes * (rows // step), one, 0, unroll=4)


def mix_kernel(coef_ref, *refs):
    pieces, outs = refs[:4], refs[4:]
    planes, half = outs[0].shape[2:4]
    for h, out_ref in enumerate(outs):

        def body(plane, at, h=h, out_ref=out_ref):
            rows = pl.ds(h * half + at, 8)
            values = [(ref[0, plane, rows, :], ref[1, plane, rows, :]) for ref in pieces]
            for e in range(4):
                real, imag = None, None
                for d in range(4):
                    c, s = coef_ref[4 * e + d], coef_ref[16 + 4 * e + d]
                    a, b = values[d]
                    re, im = a * c - b * s, a * s + b * c
                    real = re if real is None else real + re
                    imag = im if imag is None else imag + im
                out_ref[e, 0, plane, pl.ds(at, 8), :] = real
                out_ref[e, 1, plane, pl.ds(at, 8), :] = imag

        per_rows(planes, half, 8, body)


def mix(pieces, coefs):
    _, planes, quarter, columns = pieces[0].shape
    half = jax.ShapeDtypeStruct((4, 2, planes, quarter // 2, columns), F32)
    return pl.pallas_call(
        mix_kernel,
        in_specs=[SMEM] + [VMEM] * 4,
        out_specs=[VMEM] * 2,
        out_shape=[half] * 2,
        compiler_params=pltpu.CompilerParams(vmem_limit_bytes=GRANT),
        cost_estimate=estimate(128 * planes * quarter * columns, 16 * planes * quarter * columns),
        name="mix",
    )(coefs, *pieces)


def butterfly_kernel(kinds, apart, *refs):
    sides, outs = refs[2:6], refs[6:]
    groups, _, planes, half, _ = sides[0].shape
    for h, (source, at_coef, twist) in enumerate(kinds):
        coef_ref, own_ref, other_ref = refs[source], sides[2 * h], sides[2 * h + 1]
        flip, c, s = [coef_ref[at_coef + i] for i in range(3)]

        def body(plane, at):
            rows = pl.ds(at, 8)
            for e in range(groups):
                real, imag = [own_ref[e, p, plane, rows, :] * flip + other_ref[e, p, plane, rows, :] for p in range(2)]
                if twist:
                    real, imag = real * c - imag * s, real * s + imag * c
                if apart:
                    into = pl.ds(h * half + at, 8)
                    outs[e][0, plane, into, :] = real
                    outs[e][1, plane, into, :] = imag
                else:
                    outs[h][e, 0, plane, rows, :] = real
                    outs[h][e, 1, plane, rows, :] = imag

        per_rows(planes, half, 8, body)


def butterfly(own, other, kinds, coefs, apart):
    groups, _, planes, half, columns = own[0].shape
    if apart:
        shapes = [jax.ShapeDtypeStruct((2, planes, 2 * half, columns), F32)] * groups
    else:
        shapes = [jax.ShapeDtypeStruct(own[0].shape, F32)] * 2
    return list(
        pl.pallas_call(
            functools.partial(butterfly_kernel, kinds, apart),
            in_specs=[SMEM] * 2 + [VMEM] * 4,
            out_specs=[VMEM] * len(shapes),
            out_shape=shapes,
            compiler_params=pltpu.CompilerParams(vmem_limit_bytes=GRANT),
            cost_estimate=estimate(10 * own[0].size, 6 * own[0].size),
            name="butterfly",
        )(*coefs, own[0], other[0], own[1], other[1])
    )


def transformed(plane, lanes, tables, piece_refs):
    right, left = tables[:2], tables[2:]
    quarter, columns = piece_refs[0].shape[2:]
    data = [jnp.concatenate([ref[0, plane], ref[1, plane]], axis=1) for ref in piece_refs]
    mixed = dot3(halves(jnp.concatenate(data, axis=0)), [ref[...] for ref in right])
    rows = []
    for i in range(len(lanes)):
        part = mixed[i * quarter : (i + 1) * quarter]
        rows += [part[:, :columns], part[:, columns:]]
    width = 2 * quarter
    sides = [jnp.concatenate([ref[:, d * width : (d + 1) * width] for d in lanes], axis=1) for ref in left]
    return dot3(sides, halves(jnp.concatenate(rows, axis=0)))


def begin_kernel(lanes, *refs):
    base_ref = refs[-1]
    local = base_ref.shape[2]
    for plane in range(base_ref.shape[0]):
        values = transformed(plane, lanes, refs[:4], refs[4:-1])
        base_ref[plane, 0] = values[:local]
        base_ref[plane, 1] = values[local:]


def begin(pieces, lanes, tables):
    _, planes, quarter, columns = pieces[0].shape
    rows = 4 * quarter
    return pl.pallas_call(
        functools.partial(begin_kernel, lanes),
        in_specs=[VMEM] * (4 + len(lanes)),
        out_specs=VMEM,
        out_shape=jax.ShapeDtypeStruct((planes, 2, rows, columns), F32),
        compiler_params=pltpu.CompilerParams(vmem_limit_bytes=GRANT),
        cost_estimate=estimate(6 * len(lanes) * planes * rows * columns * (rows + columns), 4 * planes * rows * columns),
        name="begin",
    )(*tables, *pieces)


def finish_kernel(start, lanes, has_base, *refs):
    out_ref, done, sems = refs[-3:]
    count = len(lanes)
    planes, _, local, _ = done.shape
    copies = []
    for plane in range(planes):
        values = transformed(plane, lanes, refs[:4], refs[4 : 4 + count])
        for part in range(2):
            half = values[part * local : (part + 1) * local]
            done[plane, part] = half + refs[4 + count][plane, part] if has_base else half
        copies.append(pltpu.make_async_copy(done.at[plane], out_ref.at[:, start + plane], sems.at[plane]))
        copies[-1].start()
    for copy in copies:
        copy.wait()


def finish(pieces, lanes, base, tables, out, start, total):
    _, planes, quarter, columns = pieces[0].shape
    rows = 4 * quarter
    args = [*tables, *pieces] + ([] if base is None else [base])
    in_specs = [VMEM] * len(args)
    aliases = {}
    if out is not None:
        in_specs.append(ANY)
        aliases = {len(args): 0}
        args.append(out)
    return pl.pallas_call(
        functools.partial(finish_kernel, start, lanes, base is not None),
        in_specs=in_specs,
        out_specs=ANY,
        out_shape=jax.ShapeDtypeStruct((2, total, rows, columns), F32),
        scratch_shapes=[
            pltpu.VMEM((planes, 2, rows, columns), F32),
            pltpu.SemaphoreType.DMA((planes,)),
        ],
        input_output_aliases=aliases,
        compiler_params=pltpu.CompilerParams(vmem_limit_bytes=GRANT),
        cost_estimate=estimate(6 * len(lanes) * planes * rows * columns * (rows + columns), 4 * planes * rows * columns),
        name="finish",
    )(*args)


def host_unit(products, length):
    value = np.exp(-2j * np.pi * (np.asarray(products) % length) / length)
    return value.real, value.imag


def pair_table(count, bit):
    index = np.arange(count)
    upper = (index >> bit) & 1
    return np.stack([1 - 2 * upper, *host_unit((index % 2**bit) * upper, 2 ** (bit + 1))], axis=1)


def mix_table(count):
    index, step = np.arange(count), np.arange(4)
    part, rest = index // (count // 4), index % (count // 4)
    k = reversed_bits(part[:, None] ^ step, 2)[:, :, None]
    d = (part[:, None] ^ step)[:, None, :]
    cosine, sine = host_unit(rest[:, None, None] * k + (count // 4) * (d * k), count)
    return np.concatenate([cosine.reshape(count, 16), sine.reshape(count, 16)], axis=1)


def row_of(table, index):
    table = jnp.asarray(table, F32)
    row = lax.dynamic_slice(table, (index, jnp.uint32(0)), (1, table.shape[1]))
    return row.reshape(table.shape[1])


def chunks_of(planes):
    size = max(1, -(-planes // 3))
    return [(at, min(size, planes - at)) for at in range(0, planes, size)]


def plan_of(chunks, steps):
    events, ready, arrived = [], [], 0.1
    for i, (_, size) in enumerate(chunks):
        events.append((arrived - 0.35, "go", i, 0))
        arrived += size + 0.1
        ready.append((arrived, i, 0))
    free, last = 0.0, {}
    while ready:
        ready.sort()
        now, i, step = ready.pop(0)
        events.append((now, "node", i, step))
        if step < steps - 2:
            free = max(now + 0.25, free) + chunks[i][1] / 2
            ready.append((free, i, step + 1))
        elif step < steps - 1:
            ready.append((now + 0.3, i, step + 1))
        else:
            last[i] = now + 0.1
    for i, (_, size) in enumerate(chunks):
        arrived = max(arrived, last[i])
        events.append((arrived - 0.35, "back", i, 0))
        arrived += size + 0.1
        events.append((arrived, "end", i, 0))
    return [event[1:] for event in sorted(events)]


def shards(velocity):
    _, planes, rows, columns = velocity.shape
    z_count = lax.axis_size("gz")
    y_count = lax.axis_size("gy")
    z_bits = z_count.bit_length() - 1
    y_bits = y_count.bit_length() - 1
    stride = z_count // 4
    quarter = rows // 4
    z_index = lax.axis_index("gz").astype(jnp.uint32)
    y_index = lax.axis_index("gy").astype(jnp.uint32)
    part = z_index >> (z_bits - 2)
    peers = [part ^ d for d in range(4)]
    shifts = [reversed_bits(z_index, z_bits), reversed_bits(y_index, y_bits)]
    velocity, z_index, y_index, part, peers, shifts = lax.optimization_barrier(
        (velocity, z_index, y_index, part, peers, shifts)
    )

    chunks = chunks_of(planes)
    quarters = velocity.reshape(2, planes, 4, quarter, columns)
    received = []
    zero = jnp.uint32(0)
    for i, (start, size) in enumerate(chunks):
        shape = (2, size, 1, quarter, columns)
        at = jnp.uint32(start)
        pieces = [None] * 4
        for lanes in ((LANES[0],), (*LANES[1:], 0)) if i == 0 else ((*LANES, 0),):
            for d in lanes:
                pieces[d] = lax.dynamic_slice(quarters, (zero, at, peers[d], zero, zero), shape)[:, :, 0]
            quarters = after(quarters, [pieces[d] for d in lanes])
        received.append(pieces[:1] + [exchanged(pieces[d], "gz", d * stride) for d in range(1, 4)])

    z_steps, y_steps = list(reversed(range(z_bits - 2))), list(reversed(range(y_bits)))
    z_table = np.concatenate([mix_table(z_count)] + [pair_table(z_count, bit) for bit in z_steps], axis=1)
    y_table = np.concatenate([pair_table(y_count, bit) for bit in y_steps], axis=1)
    coefs = [row_of(z_table, z_index), row_of(y_table, y_index)]
    tables = [
        *right_tables(shifts[0].astype(jnp.int32), z_count, columns),
        *left_tables(shifts[1].astype(jnp.int32), y_count, rows, part.astype(jnp.int32)),
    ]
    z_pairs = [("gz", bit, (0, 32 + 3 * i, bit > 0)) for i, bit in enumerate(z_steps)]
    y_pairs = [("gy", bit, (1, 3 * i, bit > 0)) for i, bit in enumerate(y_steps)]
    ways = list(zip(z_pairs + y_pairs[:-1], y_pairs[:-1] + z_pairs))
    ways.append((y_pairs[-1], y_pairs[-1]))

    state = [None] * len(chunks)
    done = None
    steps = len(ways) + 1
    back = [None] * len(chunks)
    result = None
    for kind, i, step in plan_of(chunks, steps):
        if kind == "node" and step == 0:
            pieces = after(received[i], done)
            state[i] = mix(pieces, coefs[0])
        elif kind == "node":
            way = ways[step - 1]
            other = [exchanged(block, axis, 2**bit) for block, (axis, bit, _) in zip(state[i], way)]
            own, other = after((state[i], other), done)
            state[i] = butterfly(own, other, tuple(pair for _, _, pair in way), coefs, step == steps - 1)
            if step == steps - 1:
                back[i] = state[i][:1] + [exchanged(state[i][d], "gz", d * stride) for d in range(1, 4)]
        elif kind == "end":
            lanes, base = (0, 1, 2, 3), None
            if i == len(chunks) - 1:
                early, lanes = (0, 1, 3), (2,)
                pieces = after([back[i][d] for d in early], done)
                base = begin(pieces, early, tables)
                done = base
            pieces = after([back[i][d] for d in lanes], done)
            result = finish(pieces, lanes, base, tables, result, chunks[i][0], planes)
        done = result if kind == "end" else state[i] if kind == "node" else done
    return result


def solution(mesh):
    in_specs = (P(None, None, "gy", "gz"),)
    out_specs = P(None, None, "gy", "gz")
    return jax.shard_map(shards, mesh=mesh, in_specs=in_specs, out_specs=out_specs, check_vma=False)
```

```python
import functools
import math

import jax
import jax.numpy as jnp
import numpy as np
from jax import lax
from jax.experimental import pallas as pl
from jax.experimental.pallas import tpu as pltpu
from jax.sharding import PartitionSpec as P


GRANT = 16 * 2**20
LANES = (3, 2, 1)

F32 = jnp.float32
BF16 = jnp.bfloat16
SMEM = pl.BlockSpec(memory_space=pltpu.SMEM)
VMEM = pl.BlockSpec(memory_space=pltpu.VMEM)
ANY = pl.BlockSpec(memory_space=pl.ANY)


def exchanged(block, axis, mask):
    count = lax.axis_size(axis)
    return lax.ppermute(block, axis, [(i, i ^ mask) for i in range(count)])


def reversed_bits(index, bit_count):
    return sum(((index >> place) & 1) << (bit_count - 1 - place) for place in range(bit_count))


def unit(products, length):
    phase = -2.0 * math.pi * (products % length).astype(F32) / length
    return jnp.cos(phase), jnp.sin(phase)


def estimate(flops, count):
    return pl.CostEstimate(flops=flops, transcendentals=0, bytes_accessed=4 * count)


def dft_table(inputs, outputs, count, local, frequency):
    length = count * local
    turn = (inputs[1] - outputs[1]) * (length // 4)
    values = unit(inputs[0] * (frequency + count * outputs[0]) - turn, length)[0] * (1.0 / math.sqrt(length))
    high = lax.reduce_precision(values, 8, 7)
    return high.astype(BF16), (values - high).astype(BF16)


def right_tables(frequency, count, local):
    at = jnp.arange(2 * local, dtype=jnp.int32)
    at = at % local, at // local
    return dft_table([x[:, None] for x in at], [x[None, :] for x in at], count, local, frequency)


def left_tables(frequency, count, local, part):
    at = jnp.arange(2 * local, dtype=jnp.int32)
    quarter = local // 4
    row = (part ^ (at // (2 * quarter))) * quarter + at % quarter
    inputs = row[None, :], (at // quarter % 2)[None, :]
    return dft_table(inputs, [x[:, None] for x in (at % local, at // local)], count, local, frequency)


def halves(values):
    high = values.astype(BF16)
    return high, (values - high.astype(F32)).astype(BF16)


def dot3(left, right):
    def single(a, b):
        return jnp.dot(a, b, preferred_element_type=F32)

    return single(left[0], right[0]) + (single(left[1], right[0]) + single(left[0], right[1]))


def after(value, done):
    return value if done is None else lax.optimization_barrier((value, done))[0]


def per_rows(planes, rows, step, body):
    def one(at, carry):
        body(at // (rows // step), pl.multiple_of(at % (rows // step) * step, step))
        return carry

    lax.fori_loop(0, planes * (rows // step), one, 0, unroll=4)


def mix_kernel(coef_ref, *refs):
    pieces, outs = refs[:4], refs[4:]
    planes, half = outs[0].shape[2:4]
    for h, out_ref in enumerate(outs):

        def body(plane, at, h=h, out_ref=out_ref):
            rows = pl.ds(h * half + at, 8)
            values = [(ref[0, plane, rows, :], ref[1, plane, rows, :]) for ref in pieces]
            for e in range(4):
                real, imag = None, None
                for d in range(4):
                    c, s = coef_ref[4 * e + d], coef_ref[16 + 4 * e + d]
                    a, b = values[d]
                    re, im = a * c - b * s, a * s + b * c
                    real = re if real is None else real + re
                    imag = im if imag is None else imag + im
                out_ref[e, 0, plane, pl.ds(at, 8), :] = real
                out_ref[e, 1, plane, pl.ds(at, 8), :] = imag

        per_rows(planes, half, 8, body)


def mix(pieces, coefs):
    _, planes, quarter, columns = pieces[0].shape
    half = jax.ShapeDtypeStruct((4, 2, planes, quarter // 2, columns), F32)
    return pl.pallas_call(
        mix_kernel,
        in_specs=[SMEM] + [VMEM] * 4,
        out_specs=[VMEM] * 2,
        out_shape=[half] * 2,
        compiler_params=pltpu.CompilerParams(vmem_limit_bytes=GRANT),
        cost_estimate=estimate(128 * planes * quarter * columns, 16 * planes * quarter * columns),
        name="mix",
    )(coefs, *pieces)


def butterfly_kernel(kinds, apart, *refs):
    sides, outs = refs[2:6], refs[6:]
    groups, _, planes, half, _ = sides[0].shape
    for h, (source, at_coef, twist) in enumerate(kinds):
        coef_ref, own_ref, other_ref = refs[source], sides[2 * h], sides[2 * h + 1]
        flip, c, s = [coef_ref[at_coef + i] for i in range(3)]

        def body(plane, at):
            rows = pl.ds(at, 8)
            for e in range(groups):
                real, imag = [own_ref[e, p, plane, rows, :] * flip + other_ref[e, p, plane, rows, :] for p in range(2)]
                if twist:
                    real, imag = real * c - imag * s, real * s + imag * c
                if apart:
                    into = pl.ds(h * half + at, 8)
                    outs[e][0, plane, into, :] = real
                    outs[e][1, plane, into, :] = imag
                else:
                    outs[h][e, 0, plane, rows, :] = real
                    outs[h][e, 1, plane, rows, :] = imag

        per_rows(planes, half, 8, body)


def butterfly(own, other, kinds, coefs, apart):
    groups, _, planes, half, columns = own[0].shape
    if apart:
        shapes = [jax.ShapeDtypeStruct((2, planes, 2 * half, columns), F32)] * groups
    else:
        shapes = [jax.ShapeDtypeStruct(own[0].shape, F32)] * 2
    return list(
        pl.pallas_call(
            functools.partial(butterfly_kernel, kinds, apart),
            in_specs=[SMEM] * 2 + [VMEM] * 4,
            out_specs=[VMEM] * len(shapes),
            out_shape=shapes,
            compiler_params=pltpu.CompilerParams(vmem_limit_bytes=GRANT),
            cost_estimate=estimate(10 * own[0].size, 6 * own[0].size),
            name="butterfly",
        )(*coefs, own[0], other[0], own[1], other[1])
    )


def transformed(lanes, tables, piece_refs):
    right, left = tables[:2], tables[2:]
    _, planes, quarter, columns = piece_refs[0].shape
    data = [jnp.concatenate([ref[0, plane], ref[1, plane]], axis=1) for plane in range(planes) for ref in piece_refs]
    high, low = halves(jnp.concatenate(data, axis=0))
    count = high.shape[0]
    both = jnp.dot(jnp.concatenate([high, low], axis=0), right[0][...], preferred_element_type=F32)
    mixed = both[:count] + (both[count:] + jnp.dot(high, right[1][...], preferred_element_type=F32))
    width = 2 * quarter
    sides = [jnp.concatenate([ref[:, d * width : (d + 1) * width] for d in lanes], axis=1) for ref in left]
    for plane in range(planes):
        rows = []
        for i in range(len(lanes)):
            at = (plane * len(lanes) + i) * quarter
            rows += [mixed[at : at + quarter, :columns], mixed[at : at + quarter, columns:]]
        yield dot3(sides, halves(jnp.concatenate(rows, axis=0)))


def begin_kernel(lanes, *refs):
    base_ref = refs[-1]
    local = base_ref.shape[2]
    for plane, values in enumerate(transformed(lanes, refs[:4], refs[4:-1])):
        base_ref[plane, 0] = values[:local]
        base_ref[plane, 1] = values[local:]


def begin(pieces, lanes, tables):
    _, planes, quarter, columns = pieces[0].shape
    rows = 4 * quarter
    return pl.pallas_call(
        functools.partial(begin_kernel, lanes),
        in_specs=[VMEM] * (4 + len(lanes)),
        out_specs=VMEM,
        out_shape=jax.ShapeDtypeStruct((planes, 2, rows, columns), F32),
        compiler_params=pltpu.CompilerParams(vmem_limit_bytes=GRANT),
        cost_estimate=estimate(6 * len(lanes) * planes * rows * columns * (rows + columns), 4 * planes * rows * columns),
        name="begin",
    )(*tables, *pieces)


def finish_kernel(start, lanes, has_base, *refs):
    out_ref, done, sems = refs[-3:]
    count = len(lanes)
    local = done.shape[2]
    copies = []
    for plane, values in enumerate(transformed(lanes, refs[:4], refs[4 : 4 + count])):
        for part in range(2):
            half = values[part * local : (part + 1) * local]
            done[plane, part] = half + refs[4 + count][plane, part] if has_base else half
        copies.append(pltpu.make_async_copy(done.at[plane], out_ref.at[:, start + plane], sems.at[plane]))
        copies[-1].start()
    for copy in copies:
        copy.wait()


def finish(pieces, lanes, base, tables, out, start, total):
    _, planes, quarter, columns = pieces[0].shape
    rows = 4 * quarter
    args = [*tables, *pieces] + ([] if base is None else [base])
    in_specs = [VMEM] * len(args)
    aliases = {}
    if out is not None:
        in_specs.append(ANY)
        aliases = {len(args): 0}
        args.append(out)
    return pl.pallas_call(
        functools.partial(finish_kernel, start, lanes, base is not None),
        in_specs=in_specs,
        out_specs=ANY,
        out_shape=jax.ShapeDtypeStruct((2, total, rows, columns), F32),
        scratch_shapes=[
            pltpu.VMEM((planes, 2, rows, columns), F32),
            pltpu.SemaphoreType.DMA((planes,)),
        ],
        input_output_aliases=aliases,
        compiler_params=pltpu.CompilerParams(vmem_limit_bytes=GRANT),
        cost_estimate=estimate(6 * len(lanes) * planes * rows * columns * (rows + columns), 4 * planes * rows * columns),
        name="finish",
    )(*args)


def host_unit(products, length):
    value = np.exp(-2j * np.pi * (np.asarray(products) % length) / length)
    return value.real, value.imag


def pair_table(count, bit):
    index = np.arange(count)
    upper = (index >> bit) & 1
    return np.stack([1 - 2 * upper, *host_unit((index % 2**bit) * upper, 2 ** (bit + 1))], axis=1)


def mix_table(count):
    index, step = np.arange(count), np.arange(4)
    part, rest = index // (count // 4), index % (count // 4)
    k = reversed_bits(part[:, None] ^ step, 2)[:, :, None]
    d = (part[:, None] ^ step)[:, None, :]
    cosine, sine = host_unit(rest[:, None, None] * k + (count // 4) * (d * k), count)
    return np.concatenate([cosine.reshape(count, 16), sine.reshape(count, 16)], axis=1)


def row_of(table, index):
    table = jnp.asarray(table, F32)
    row = lax.dynamic_slice(table, (index, jnp.uint32(0)), (1, table.shape[1]))
    return row.reshape(table.shape[1])


def chunks_of(planes):
    size = max(1, -(-planes // 3))
    return [(at, min(size, planes - at)) for at in range(0, planes, size)]


def plan_of(chunks, steps):
    events, ready, arrived = [], [], 0.1
    for i, (_, size) in enumerate(chunks):
        events.append((arrived - 0.35, "go", i, 0))
        arrived += size + 0.1
        ready.append((arrived, i, 0))
    free, last = 0.0, {}
    while ready:
        ready.sort()
        now, i, step = ready.pop(0)
        events.append((now, "node", i, step))
        if step < steps - 2:
            free = max(now + 0.25, free) + chunks[i][1] / 2
            ready.append((free, i, step + 1))
        elif step < steps - 1:
            ready.append((now + 0.3, i, step + 1))
        else:
            last[i] = now + 0.1
    for i, (_, size) in enumerate(chunks):
        arrived = max(arrived, last[i])
        events.append((arrived - 0.35, "back", i, 0))
        arrived += size + 0.1
        events.append((arrived, "end", i, 0))
    return [event[1:] for event in sorted(events)]


def shards(velocity):
    _, planes, rows, columns = velocity.shape
    z_count = lax.axis_size("gz")
    y_count = lax.axis_size("gy")
    z_bits = z_count.bit_length() - 1
    y_bits = y_count.bit_length() - 1
    stride = z_count // 4
    quarter = rows // 4
    z_index = lax.axis_index("gz").astype(jnp.uint32)
    y_index = lax.axis_index("gy").astype(jnp.uint32)
    part = z_index >> (z_bits - 2)
    peers = [part ^ d for d in range(4)]
    shifts = [reversed_bits(z_index, z_bits), reversed_bits(y_index, y_bits)]
    velocity, z_index, y_index, part, peers, shifts = lax.optimization_barrier(
        (velocity, z_index, y_index, part, peers, shifts)
    )

    chunks = chunks_of(planes)
    quarters = velocity.reshape(2, planes, 4, quarter, columns)
    received = []
    zero = jnp.uint32(0)
    for i, (start, size) in enumerate(chunks):
        shape = (2, size, 1, quarter, columns)
        at = jnp.uint32(start)
        pieces = [None] * 4
        for lanes in (LANES, (0,)) if i == 0 else ((*LANES, 0),):
            for d in lanes:
                pieces[d] = lax.dynamic_slice(quarters, (zero, at, peers[d], zero, zero), shape)[:, :, 0]
            quarters = after(quarters, [pieces[d] for d in lanes])
        received.append(pieces[:1] + [exchanged(pieces[d], "gz", d * stride) for d in range(1, 4)])

    z_steps, y_steps = list(reversed(range(z_bits - 2))), list(reversed(range(y_bits)))
    z_table = np.concatenate([mix_table(z_count)] + [pair_table(z_count, bit) for bit in z_steps], axis=1)
    y_table = np.concatenate([pair_table(y_count, bit) for bit in y_steps], axis=1)
    coefs = [row_of(z_table, z_index), row_of(y_table, y_index)]
    tables = [
        *right_tables(shifts[0].astype(jnp.int32), z_count, columns),
        *left_tables(shifts[1].astype(jnp.int32), y_count, rows, part.astype(jnp.int32)),
    ]
    z_pairs = [("gz", bit, (0, 32 + 3 * i, bit > 0)) for i, bit in enumerate(z_steps)]
    y_pairs = [("gy", bit, (1, 3 * i, bit > 0)) for i, bit in enumerate(y_steps)]
    ways = list(zip(z_pairs + y_pairs[:-1], y_pairs[:-1] + z_pairs))
    ways.append((y_pairs[-1], y_pairs[-1]))

    state = [None] * len(chunks)
    done = None
    steps = len(ways) + 1
    back = [None] * len(chunks)
    result = None
    for kind, i, step in plan_of(chunks, steps):
        if kind == "node" and step == 0:
            pieces = after(received[i], done)
            state[i] = mix(pieces, coefs[0])
        elif kind == "node":
            way = ways[step - 1]
            other = [exchanged(block, axis, 2**bit) for block, (axis, bit, _) in zip(state[i], way)]
            own, other = after((state[i], other), done)
            state[i] = butterfly(own, other, tuple(pair for _, _, pair in way), coefs, step == steps - 1)
            if step == steps - 1:
                back[i] = state[i][:1] + [exchanged(state[i][d], "gz", d * stride) for d in range(1, 4)]
        elif kind == "end":
            lanes, base = (0, 1, 2, 3), None
            if i == len(chunks) - 1:
                early, lanes = (0, 1, 3), (2,)
                pieces = after([back[i][d] for d in early], done)
                base = begin(pieces, early, tables)
                done = base
            pieces = after([back[i][d] for d in lanes], done)
            result = finish(pieces, lanes, base, tables, result, chunks[i][0], planes)
        done = result if kind == "end" else state[i] if kind == "node" else done
    return result


def solution(mesh):
    in_specs = (P(None, None, "gy", "gz"),)
    out_specs = P(None, None, "gy", "gz")
    return jax.shard_map(shards, mesh=mesh, in_specs=in_specs, out_specs=out_specs, check_vma=False)
```

```python
import functools
import math

import jax
import jax.numpy as jnp
import numpy as np
from jax import lax
from jax.experimental import pallas as pl
from jax.experimental.pallas import tpu as pltpu
from jax.sharding import PartitionSpec as P


GRANT = 16 * 2**20
LANES = (3, 2, 1)

F32 = jnp.float32
BF16 = jnp.bfloat16
SMEM = pl.BlockSpec(memory_space=pltpu.SMEM)
VMEM = pl.BlockSpec(memory_space=pltpu.VMEM)
ANY = pl.BlockSpec(memory_space=pl.ANY)


def exchanged(block, axis, mask):
    count = lax.axis_size(axis)
    return lax.ppermute(block, axis, [(i, i ^ mask) for i in range(count)])


def reversed_bits(index, bit_count):
    return sum(((index >> place) & 1) << (bit_count - 1 - place) for place in range(bit_count))


def unit(products, length):
    phase = -2.0 * math.pi * (products % length).astype(F32) / length
    return jnp.cos(phase), jnp.sin(phase)


def estimate(flops, count):
    return pl.CostEstimate(flops=flops, transcendentals=0, bytes_accessed=4 * count)


def dft_table(inputs, outputs, count, local, frequency):
    length = count * local
    turn = (inputs[1] - outputs[1]) * (length // 4)
    values = unit(inputs[0] * (frequency + count * outputs[0]) - turn, length)[0] * (1.0 / math.sqrt(length))
    high = lax.reduce_precision(values, 8, 7)
    return high.astype(BF16), (values - high).astype(BF16)


def right_tables(frequency, count, local):
    at = jnp.arange(2 * local, dtype=jnp.int32)
    at = at % local, at // local
    return dft_table([x[:, None] for x in at], [x[None, :] for x in at], count, local, frequency)


def left_tables(frequency, count, local, part):
    at = jnp.arange(2 * local, dtype=jnp.int32)
    quarter = local // 4
    row = (part ^ (at // (2 * quarter))) * quarter + at % quarter
    inputs = row[None, :], (at // quarter % 2)[None, :]
    return dft_table(inputs, [x[:, None] for x in (at % local, at // local)], count, local, frequency)


def halves(values):
    high = values.astype(BF16)
    return high, (values - high.astype(F32)).astype(BF16)


def dot3(left, right):
    def single(a, b):
        return jnp.dot(a, b, preferred_element_type=F32)

    return single(left[0], right[0]) + (single(left[1], right[0]) + single(left[0], right[1]))


def after(value, done):
    return value if done is None else lax.optimization_barrier((value, done))[0]


def per_rows(planes, rows, step, body):
    def one(at, carry):
        body(at // (rows // step), pl.multiple_of(at % (rows // step) * step, step))
        return carry

    lax.fori_loop(0, planes * (rows // step), one, 0, unroll=4)


def pack_kernel(stride, x_ref, *refs):
    outs, sems = refs[:-1], refs[-1]
    _, planes, quarter, _ = outs[0].shape
    part = lax.axis_index("gz") // stride
    copies = []
    for d in (*LANES, 0):
        rows = pl.ds(pl.multiple_of((part ^ d) * quarter, quarter), quarter)
        copies.append(pltpu.make_async_copy(x_ref.at[:, pl.ds(0, planes), rows, :], outs[d], sems.at[d]))
        copies[-1].start()
    for copy in copies:
        copy.wait()


def pack(x, stride, planes):
    _, _, rows, columns = x.shape
    piece = jax.ShapeDtypeStruct((2, planes, rows // 4, columns), F32)
    return list(
        pl.pallas_call(
            functools.partial(pack_kernel, stride),
            in_specs=[ANY],
            out_specs=[VMEM] * 4,
            out_shape=[pltpu.VMEM(piece.shape, F32)] * 4,
            scratch_shapes=[pltpu.SemaphoreType.DMA((4,))],
            compiler_params=pltpu.CompilerParams(vmem_limit_bytes=GRANT),
            cost_estimate=estimate(0, 4 * planes * rows * columns),
            name="pack",
        )(pltpu.with_memory_space_constraint(x, pltpu.HBM))
    )


def mix_kernel(coef_ref, *refs):
    pieces, outs = refs[:4], refs[4:]
    planes, half = outs[0].shape[2:4]
    for h, out_ref in enumerate(outs):

        def body(plane, at, h=h, out_ref=out_ref):
            rows = pl.ds(h * half + at, 8)
            values = [(ref[0, plane, rows, :], ref[1, plane, rows, :]) for ref in pieces]
            for e in range(4):
                real, imag = None, None
                for d in range(4):
                    c, s = coef_ref[4 * e + d], coef_ref[16 + 4 * e + d]
                    a, b = values[d]
                    re, im = a * c - b * s, a * s + b * c
                    real = re if real is None else real + re
                    imag = im if imag is None else imag + im
                out_ref[e, 0, plane, pl.ds(at, 8), :] = real
                out_ref[e, 1, plane, pl.ds(at, 8), :] = imag

        per_rows(planes, half, 8, body)


def mix(pieces, coefs):
    _, planes, quarter, columns = pieces[0].shape
    half = jax.ShapeDtypeStruct((4, 2, planes, quarter // 2, columns), F32)
    return pl.pallas_call(
        mix_kernel,
        in_specs=[SMEM] + [VMEM] * 4,
        out_specs=[VMEM] * 2,
        out_shape=[half] * 2,
        compiler_params=pltpu.CompilerParams(vmem_limit_bytes=GRANT),
        cost_estimate=estimate(128 * planes * quarter * columns, 16 * planes * quarter * columns),
        name="mix",
    )(coefs, *pieces)


def butterfly_kernel(kinds, apart, *refs):
    sides, outs = refs[2:6], refs[6:]
    groups, _, planes, half, _ = sides[0].shape
    for h, (source, at_coef, twist) in enumerate(kinds):
        coef_ref, own_ref, other_ref = refs[source], sides[2 * h], sides[2 * h + 1]
        flip, c, s = [coef_ref[at_coef + i] for i in range(3)]

        def body(plane, at):
            rows = pl.ds(at, 8)
            for e in range(groups):
                real, imag = [own_ref[e, p, plane, rows, :] * flip + other_ref[e, p, plane, rows, :] for p in range(2)]
                if twist:
                    real, imag = real * c - imag * s, real * s + imag * c
                if apart:
                    into = pl.ds(h * half + at, 8)
                    outs[e][0, plane, into, :] = real
                    outs[e][1, plane, into, :] = imag
                else:
                    outs[h][e, 0, plane, rows, :] = real
                    outs[h][e, 1, plane, rows, :] = imag

        per_rows(planes, half, 8, body)


def butterfly(own, other, kinds, coefs, apart):
    groups, _, planes, half, columns = own[0].shape
    if apart:
        shapes = [jax.ShapeDtypeStruct((2, planes, 2 * half, columns), F32)] * groups
    else:
        shapes = [jax.ShapeDtypeStruct(own[0].shape, F32)] * 2
    return list(
        pl.pallas_call(
            functools.partial(butterfly_kernel, kinds, apart),
            in_specs=[SMEM] * 2 + [VMEM] * 4,
            out_specs=[VMEM] * len(shapes),
            out_shape=shapes,
            compiler_params=pltpu.CompilerParams(vmem_limit_bytes=GRANT),
            cost_estimate=estimate(10 * own[0].size, 6 * own[0].size),
            name="butterfly",
        )(*coefs, own[0], other[0], own[1], other[1])
    )


def transformed(lanes, tables, piece_refs):
    right, left = tables[:2], tables[2:]
    _, planes, quarter, columns = piece_refs[0].shape
    data = [jnp.concatenate([ref[0, plane], ref[1, plane]], axis=1) for plane in range(planes) for ref in piece_refs]
    high, low = halves(jnp.concatenate(data, axis=0))
    count = high.shape[0]
    both = jnp.dot(jnp.concatenate([high, low], axis=0), right[0][...], preferred_element_type=F32)
    mixed = both[:count] + (both[count:] + jnp.dot(high, right[1][...], preferred_element_type=F32))
    width = 2 * quarter
    sides = [jnp.concatenate([ref[:, d * width : (d + 1) * width] for d in lanes], axis=1) for ref in left]
    for plane in range(planes):
        rows = []
        for i in range(len(lanes)):
            at = (plane * len(lanes) + i) * quarter
            rows += [mixed[at : at + quarter, :columns], mixed[at : at + quarter, columns:]]
        yield dot3(sides, halves(jnp.concatenate(rows, axis=0)))


def begin_kernel(lanes, *refs):
    base_ref = refs[-1]
    local = base_ref.shape[2]
    for plane, values in enumerate(transformed(lanes, refs[:4], refs[4:-1])):
        base_ref[plane, 0] = values[:local]
        base_ref[plane, 1] = values[local:]


def begin(pieces, lanes, tables):
    _, planes, quarter, columns = pieces[0].shape
    rows = 4 * quarter
    return pl.pallas_call(
        functools.partial(begin_kernel, lanes),
        in_specs=[VMEM] * (4 + len(lanes)),
        out_specs=VMEM,
        out_shape=jax.ShapeDtypeStruct((planes, 2, rows, columns), F32),
        compiler_params=pltpu.CompilerParams(vmem_limit_bytes=GRANT),
        cost_estimate=estimate(6 * len(lanes) * planes * rows * columns * (rows + columns), 4 * planes * rows * columns),
        name="begin",
    )(*tables, *pieces)


def finish_kernel(start, lanes, has_base, *refs):
    out_ref, done, sems = refs[-3:]
    count = len(lanes)
    local = done.shape[2]
    copies = []
    for plane, values in enumerate(transformed(lanes, refs[:4], refs[4 : 4 + count])):
        for part in range(2):
            half = values[part * local : (part + 1) * local]
            done[plane, part] = half + refs[4 + count][plane, part] if has_base else half
        copies.append(pltpu.make_async_copy(done.at[plane], out_ref.at[:, start + plane], sems.at[plane]))
        copies[-1].start()
    for copy in copies:
        copy.wait()


def finish(pieces, lanes, base, tables, out, start, total):
    _, planes, quarter, columns = pieces[0].shape
    rows = 4 * quarter
    args = [*tables, *pieces] + ([] if base is None else [base])
    in_specs = [VMEM] * len(args)
    aliases = {}
    if out is not None:
        in_specs.append(ANY)
        aliases = {len(args): 0}
        args.append(out)
    return pl.pallas_call(
        functools.partial(finish_kernel, start, lanes, base is not None),
        in_specs=in_specs,
        out_specs=ANY,
        out_shape=jax.ShapeDtypeStruct((2, total, rows, columns), F32),
        scratch_shapes=[
            pltpu.VMEM((planes, 2, rows, columns), F32),
            pltpu.SemaphoreType.DMA((planes,)),
        ],
        input_output_aliases=aliases,
        compiler_params=pltpu.CompilerParams(vmem_limit_bytes=GRANT),
        cost_estimate=estimate(6 * len(lanes) * planes * rows * columns * (rows + columns), 4 * planes * rows * columns),
        name="finish",
    )(*args)


def host_unit(products, length):
    value = np.exp(-2j * np.pi * (np.asarray(products) % length) / length)
    return value.real, value.imag


def pair_table(count, bit):
    index = np.arange(count)
    upper = (index >> bit) & 1
    return np.stack([1 - 2 * upper, *host_unit((index % 2**bit) * upper, 2 ** (bit + 1))], axis=1)


def mix_table(count):
    index, step = np.arange(count), np.arange(4)
    part, rest = index // (count // 4), index % (count // 4)
    k = reversed_bits(part[:, None] ^ step, 2)[:, :, None]
    d = (part[:, None] ^ step)[:, None, :]
    cosine, sine = host_unit(rest[:, None, None] * k + (count // 4) * (d * k), count)
    return np.concatenate([cosine.reshape(count, 16), sine.reshape(count, 16)], axis=1)


def row_of(table, index):
    table = jnp.asarray(table, F32)
    row = lax.dynamic_slice(table, (index, jnp.uint32(0)), (1, table.shape[1]))
    return row.reshape(table.shape[1])


def chunks_of(planes):
    size = max(1, -(-planes // 3))
    return [(at, min(size, planes - at)) for at in range(0, planes, size)]


def plan_of(chunks, steps):
    events, ready, arrived = [], [], 0.1
    for i, (_, size) in enumerate(chunks):
        events.append((arrived - 0.35, "go", i, 0))
        arrived += size + 0.1
        ready.append((arrived, i, 0))
    free, last = 0.0, {}
    while ready:
        ready.sort()
        now, i, step = ready.pop(0)
        events.append((now, "node", i, step))
        if step < steps - 2:
            free = max(now + 0.25, free) + chunks[i][1] / 2
            ready.append((free, i, step + 1))
        elif step < steps - 1:
            ready.append((now + 0.3, i, step + 1))
        else:
            last[i] = now + 0.1
    for i, (_, size) in enumerate(chunks):
        arrived = max(arrived, last[i])
        events.append((arrived - 0.35, "back", i, 0))
        arrived += size + 0.1
        events.append((arrived, "end", i, 0))
    return [event[1:] for event in sorted(events)]


def shards(velocity):
    _, planes, rows, columns = velocity.shape
    z_count = lax.axis_size("gz")
    y_count = lax.axis_size("gy")
    z_bits = z_count.bit_length() - 1
    y_bits = y_count.bit_length() - 1
    stride = z_count // 4
    quarter = rows // 4
    z_index = lax.axis_index("gz").astype(jnp.uint32)
    y_index = lax.axis_index("gy").astype(jnp.uint32)
    part = z_index >> (z_bits - 2)
    peers = [part ^ d for d in range(4)]
    shifts = [reversed_bits(z_index, z_bits), reversed_bits(y_index, y_bits)]
    velocity, z_index, y_index, part, peers, shifts = lax.optimization_barrier(
        (velocity, z_index, y_index, part, peers, shifts)
    )

    chunks = chunks_of(planes)
    quarters = velocity.reshape(2, planes, 4, quarter, columns)
    received = []
    zero = jnp.uint32(0)
    for i, (start, size) in enumerate(chunks):
        shape = (2, size, 1, quarter, columns)
        at = jnp.uint32(start)
        if i == 0:
            pieces = pack(velocity, stride, size)
        else:
            pieces = [lax.dynamic_slice(quarters, (zero, at, peer, zero, zero), shape)[:, :, 0] for peer in peers]
        quarters = after(quarters, pieces)
        received.append(pieces[:1] + [exchanged(pieces[d], "gz", d * stride) for d in range(1, 4)])

    z_steps, y_steps = list(reversed(range(z_bits - 2))), list(reversed(range(y_bits)))
    z_table = np.concatenate([mix_table(z_count)] + [pair_table(z_count, bit) for bit in z_steps], axis=1)
    y_table = np.concatenate([pair_table(y_count, bit) for bit in y_steps], axis=1)
    coefs = [row_of(z_table, z_index), row_of(y_table, y_index)]
    tables = [
        *right_tables(shifts[0].astype(jnp.int32), z_count, columns),
        *left_tables(shifts[1].astype(jnp.int32), y_count, rows, part.astype(jnp.int32)),
    ]
    z_pairs = [("gz", bit, (0, 32 + 3 * i, bit > 0)) for i, bit in enumerate(z_steps)]
    y_pairs = [("gy", bit, (1, 3 * i, bit > 0)) for i, bit in enumerate(y_steps)]
    ways = list(zip(z_pairs + y_pairs[:-1], y_pairs[:-1] + z_pairs))
    ways.append((y_pairs[-1], y_pairs[-1]))

    state = [None] * len(chunks)
    done = None
    steps = len(ways) + 1
    back = [None] * len(chunks)
    result = None
    for kind, i, step in plan_of(chunks, steps):
        if kind == "node" and step == 0:
            pieces = after(received[i], done)
            state[i] = mix(pieces, coefs[0])
        elif kind == "node":
            way = ways[step - 1]
            other = [exchanged(block, axis, 2**bit) for block, (axis, bit, _) in zip(state[i], way)]
            own, other = after((state[i], other), done)
            state[i] = butterfly(own, other, tuple(pair for _, _, pair in way), coefs, step == steps - 1)
            if step == steps - 1:
                back[i] = state[i][:1] + [exchanged(state[i][d], "gz", d * stride) for d in range(1, 4)]
        elif kind == "end":
            lanes, base = (0, 1, 2, 3), None
            if i == len(chunks) - 1:
                early, lanes = (0, 1, 3), (2,)
                pieces = after([back[i][d] for d in early], done)
                base = begin(pieces, early, tables)
                done = base
            pieces = after([back[i][d] for d in lanes], done)
            result = finish(pieces, lanes, base, tables, result, chunks[i][0], planes)
        done = result if kind == "end" else state[i] if kind == "node" else done
    return result


def solution(mesh):
    in_specs = (P(None, None, "gy", "gz"),)
    out_specs = P(None, None, "gy", "gz")
    return jax.shard_map(shards, mesh=mesh, in_specs=in_specs, out_specs=out_specs, check_vma=False)
```

```python
import functools
import math

import jax
import jax.numpy as jnp
import numpy as np
from jax import lax
from jax.experimental import pallas as pl
from jax.experimental.pallas import tpu as pltpu
from jax.sharding import PartitionSpec as P


GRANT = 16 * 2**20
LANES = (2, 3, 1)

F32 = jnp.float32
BF16 = jnp.bfloat16
SMEM = pl.BlockSpec(memory_space=pltpu.SMEM)
VMEM = pl.BlockSpec(memory_space=pltpu.VMEM)
ANY = pl.BlockSpec(memory_space=pl.ANY)


def exchanged(block, axis, mask):
    count = lax.axis_size(axis)
    return lax.ppermute(block, axis, [(i, i ^ mask) for i in range(count)])


def reversed_bits(index, bit_count):
    return sum(((index >> place) & 1) << (bit_count - 1 - place) for place in range(bit_count))


def unit(products, length):
    phase = -2.0 * math.pi * (products % length).astype(F32) / length
    return jnp.cos(phase), jnp.sin(phase)


def estimate(flops, count):
    return pl.CostEstimate(flops=flops, transcendentals=0, bytes_accessed=4 * count)


def dft_table(inputs, outputs, count, local, frequency):
    length = count * local
    turn = (inputs[1] - outputs[1]) * (length // 4)
    values = unit(inputs[0] * (frequency + count * outputs[0]) - turn, length)[0] * (1.0 / math.sqrt(length))
    high = lax.reduce_precision(values, 8, 7)
    return high.astype(BF16), (values - high).astype(BF16)


def right_tables(frequency, count, local):
    at = jnp.arange(2 * local, dtype=jnp.int32)
    at = at % local, at // local
    return dft_table([x[:, None] for x in at], [x[None, :] for x in at], count, local, frequency)


def left_tables(frequency, count, local, part):
    at = jnp.arange(2 * local, dtype=jnp.int32)
    quarter = local // 4
    row = (part ^ (at // (2 * quarter))) * quarter + at % quarter
    inputs = row[None, :], (at // quarter % 2)[None, :]
    return dft_table(inputs, [x[:, None] for x in (at % local, at // local)], count, local, frequency)


def halves(values):
    high = values.astype(BF16)
    return high, (values - high.astype(F32)).astype(BF16)


def dot3(left, right):
    def single(a, b):
        return jnp.dot(a, b, preferred_element_type=F32)

    return single(left[0], right[0]) + (single(left[1], right[0]) + single(left[0], right[1]))


def after(value, done):
    return value if done is None else lax.optimization_barrier((value, done))[0]


def per_rows(planes, rows, step, body):
    def one(at, carry):
        body(at // (rows // step), pl.multiple_of(at % (rows // step) * step, step))
        return carry

    lax.fori_loop(0, planes * (rows // step), one, 0, unroll=4)


def mix_kernel(coef_ref, *refs):
    pieces, outs = refs[:4], refs[4:]
    planes, half = outs[0].shape[2:4]
    for h, out_ref in enumerate(outs):

        def body(plane, at, h=h, out_ref=out_ref):
            rows = pl.ds(h * half + at, 8)
            values = [(ref[0, plane, rows, :], ref[1, plane, rows, :]) for ref in pieces]
            for e in range(4):
                real, imag = None, None
                for d in range(4):
                    c, s = coef_ref[4 * e + d], coef_ref[16 + 4 * e + d]
                    a, b = values[d]
                    re, im = a * c - b * s, a * s + b * c
                    real = re if real is None else real + re
                    imag = im if imag is None else imag + im
                out_ref[e, 0, plane, pl.ds(at, 8), :] = real
                out_ref[e, 1, plane, pl.ds(at, 8), :] = imag

        per_rows(planes, half, 8, body)


def mix(pieces, coefs):
    _, planes, quarter, columns = pieces[0].shape
    half = jax.ShapeDtypeStruct((4, 2, planes, quarter // 2, columns), F32)
    return pl.pallas_call(
        mix_kernel,
        in_specs=[SMEM] + [VMEM] * 4,
        out_specs=[VMEM] * 2,
        out_shape=[half] * 2,
        compiler_params=pltpu.CompilerParams(vmem_limit_bytes=GRANT),
        cost_estimate=estimate(128 * planes * quarter * columns, 16 * planes * quarter * columns),
        name="mix",
    )(coefs, *pieces)


def butterfly_kernel(kinds, apart, *refs):
    sides, outs = refs[2:6], refs[6:]
    groups, _, planes, half, _ = sides[0].shape
    for h, (source, at_coef, twist) in enumerate(kinds):
        coef_ref, own_ref, other_ref = refs[source], sides[2 * h], sides[2 * h + 1]
        flip, c, s = [coef_ref[at_coef + i] for i in range(3)]

        def body(plane, at):
            rows = pl.ds(at, 8)
            for e in range(groups):
                real, imag = [own_ref[e, p, plane, rows, :] * flip + other_ref[e, p, plane, rows, :] for p in range(2)]
                if twist:
                    real, imag = real * c - imag * s, real * s + imag * c
                if apart:
                    into = pl.ds(h * half + at, 8)
                    outs[e][0, plane, into, :] = real
                    outs[e][1, plane, into, :] = imag
                else:
                    outs[h][e, 0, plane, rows, :] = real
                    outs[h][e, 1, plane, rows, :] = imag

        per_rows(planes, half, 8, body)


def butterfly(own, other, kinds, coefs, apart):
    groups, _, planes, half, columns = own[0].shape
    if apart:
        shapes = [jax.ShapeDtypeStruct((2, planes, 2 * half, columns), F32)] * groups
    else:
        shapes = [jax.ShapeDtypeStruct(own[0].shape, F32)] * 2
    return list(
        pl.pallas_call(
            functools.partial(butterfly_kernel, kinds, apart),
            in_specs=[SMEM] * 2 + [VMEM] * 4,
            out_specs=[VMEM] * len(shapes),
            out_shape=shapes,
            compiler_params=pltpu.CompilerParams(vmem_limit_bytes=GRANT),
            cost_estimate=estimate(10 * own[0].size, 6 * own[0].size),
            name="butterfly",
        )(*coefs, own[0], other[0], own[1], other[1])
    )


def transformed(lanes, tables, piece_refs):
    right, left = tables[:2], tables[2:]
    _, planes, quarter, columns = piece_refs[0].shape
    data = [jnp.concatenate([ref[0, plane], ref[1, plane]], axis=1) for plane in range(planes) for ref in piece_refs]
    high, low = halves(jnp.concatenate(data, axis=0))
    count = high.shape[0]
    both = jnp.dot(jnp.concatenate([high, low], axis=0), right[0][...], preferred_element_type=F32)
    mixed = both[:count] + (both[count:] + jnp.dot(high, right[1][...], preferred_element_type=F32))
    width, local = 2 * quarter, 4 * quarter
    for plane in range(planes):
        rows = []
        for i in range(len(lanes)):
            at = (plane * len(lanes) + i) * quarter
            rows += [mixed[at : at + quarter, :columns], mixed[at : at + quarter, columns:]]
        rows = halves(jnp.concatenate(rows, axis=0))
        for part in range(2):
            at = slice(part * local, (part + 1) * local)
            sides = [jnp.concatenate([ref[at, d * width : (d + 1) * width] for d in lanes], axis=1) for ref in left]
            yield plane, part, dot3(sides, rows)


def begin_kernel(lanes, *refs):
    for plane, part, values in transformed(lanes, refs[:4], refs[4:-1]):
        refs[-1][plane, part] = values


def begin(pieces, lanes, tables):
    _, planes, quarter, columns = pieces[0].shape
    rows = 4 * quarter
    return pl.pallas_call(
        functools.partial(begin_kernel, lanes),
        in_specs=[VMEM] * (4 + len(lanes)),
        out_specs=VMEM,
        out_shape=jax.ShapeDtypeStruct((planes, 2, rows, columns), F32),
        compiler_params=pltpu.CompilerParams(vmem_limit_bytes=GRANT),
        cost_estimate=estimate(6 * len(lanes) * planes * rows * columns * (rows + columns), 4 * planes * rows * columns),
        name="begin",
    )(*tables, *pieces)


def finish_kernel(start, lanes, has_base, *refs):
    out_ref, done, sems = refs[-3:]
    count = len(lanes)
    copies = []
    for plane, part, values in transformed(lanes, refs[:4], refs[4 : 4 + count]):
        done[plane, part] = values + refs[4 + count][plane, part] if has_base else values
        copies.append(pltpu.make_async_copy(done.at[plane, part], out_ref.at[part, start + plane], sems.at[plane, part]))
        copies[-1].start()
    for copy in copies:
        copy.wait()


def finish(pieces, lanes, base, tables, out, start, total):
    _, planes, quarter, columns = pieces[0].shape
    rows = 4 * quarter
    args = [*tables, *pieces] + ([] if base is None else [base])
    in_specs = [VMEM] * len(args)
    aliases = {}
    if out is not None:
        in_specs.append(ANY)
        aliases = {len(args): 0}
        args.append(out)
    return pl.pallas_call(
        functools.partial(finish_kernel, start, lanes, base is not None),
        in_specs=in_specs,
        out_specs=ANY,
        out_shape=jax.ShapeDtypeStruct((2, total, rows, columns), F32),
        scratch_shapes=[
            pltpu.VMEM((planes, 2, rows, columns), F32),
            pltpu.SemaphoreType.DMA((planes, 2)),
        ],
        input_output_aliases=aliases,
        compiler_params=pltpu.CompilerParams(vmem_limit_bytes=GRANT),
        cost_estimate=estimate(6 * len(lanes) * planes * rows * columns * (rows + columns), 4 * planes * rows * columns),
        name="finish",
    )(*args)


def host_unit(products, length):
    value = np.exp(-2j * np.pi * (np.asarray(products) % length) / length)
    return value.real, value.imag


def pair_table(count, bit):
    index = np.arange(count)
    upper = (index >> bit) & 1
    return np.stack([1 - 2 * upper, *host_unit((index % 2**bit) * upper, 2 ** (bit + 1))], axis=1)


def mix_table(count):
    index, step = np.arange(count), np.arange(4)
    part, rest = index // (count // 4), index % (count // 4)
    k = reversed_bits(part[:, None] ^ step, 2)[:, :, None]
    d = (part[:, None] ^ step)[:, None, :]
    cosine, sine = host_unit(rest[:, None, None] * k + (count // 4) * (d * k), count)
    return np.concatenate([cosine.reshape(count, 16), sine.reshape(count, 16)], axis=1)


def row_of(table, index):
    table = jnp.asarray(table, F32)
    row = lax.dynamic_slice(table, (index, jnp.uint32(0)), (1, table.shape[1]))
    return row.reshape(table.shape[1])


def chunks_of(planes):
    size = max(1, -(-planes // 3))
    return [(at, min(size, planes - at)) for at in range(0, planes, size)]


def plan_of(chunks, steps):
    events, ready, arrived = [], [], 0.1
    for i, (_, size) in enumerate(chunks):
        events.append((arrived - 0.35, "go", i, 0))
        arrived += size + 0.1
        ready.append((arrived, i, 0))
    free, last = 0.0, {}
    while ready:
        ready.sort()
        now, i, step = ready.pop(0)
        events.append((now, "node", i, step))
        if step < steps - 2:
            free = max(now + 0.25, free) + chunks[i][1] / 2
            ready.append((free, i, step + 1))
        elif step < steps - 1:
            ready.append((now + 0.3, i, step + 1))
        else:
            last[i] = now + 0.1
    for i, (_, size) in enumerate(chunks):
        arrived = max(arrived, last[i])
        events.append((arrived - 0.35, "back", i, 0))
        arrived += size + 0.1
        events.append((arrived, "end", i, 0))
    return [event[1:] for event in sorted(events)]


def shards(velocity):
    _, planes, rows, columns = velocity.shape
    z_count = lax.axis_size("gz")
    y_count = lax.axis_size("gy")
    z_bits = z_count.bit_length() - 1
    y_bits = y_count.bit_length() - 1
    stride = z_count // 4
    quarter = rows // 4
    z_index = lax.axis_index("gz").astype(jnp.uint32)
    y_index = lax.axis_index("gy").astype(jnp.uint32)
    part = z_index >> (z_bits - 2)
    peers = [part ^ d for d in range(4)]
    shifts = [reversed_bits(z_index, z_bits), reversed_bits(y_index, y_bits)]
    velocity, z_index, y_index, part, peers, shifts = lax.optimization_barrier(
        (velocity, z_index, y_index, part, peers, shifts)
    )

    chunks = chunks_of(planes)
    quarters = velocity.reshape(2, planes, 4, quarter, columns)
    received = []
    zero = jnp.uint32(0)
    for i, (start, size) in enumerate(chunks):
        shape = (2, size, 1, quarter, columns)
        at = jnp.uint32(start)
        pieces = [None] * 4
        for lanes in ((LANES[0],), (*LANES[1:], 0)) if i == 0 else ((*LANES, 0),):
            for d in lanes:
                pieces[d] = lax.dynamic_slice(quarters, (zero, at, peers[d], zero, zero), shape)[:, :, 0]
            quarters = after(quarters, [pieces[d] for d in lanes])
        received.append(pieces[:1] + [exchanged(pieces[d], "gz", d * stride) for d in range(1, 4)])

    z_steps, y_steps = list(reversed(range(z_bits - 2))), list(reversed(range(y_bits)))
    z_table = np.concatenate([mix_table(z_count)] + [pair_table(z_count, bit) for bit in z_steps], axis=1)
    y_table = np.concatenate([pair_table(y_count, bit) for bit in y_steps], axis=1)
    coefs = [row_of(z_table, z_index), row_of(y_table, y_index)]
    tables = [
        *right_tables(shifts[0].astype(jnp.int32), z_count, columns),
        *left_tables(shifts[1].astype(jnp.int32), y_count, rows, part.astype(jnp.int32)),
    ]
    z_pairs = [("gz", bit, (0, 32 + 3 * i, bit > 0)) for i, bit in enumerate(z_steps)]
    y_pairs = [("gy", bit, (1, 3 * i, bit > 0)) for i, bit in enumerate(y_steps)]
    ways = list(zip(z_pairs + y_pairs[:-1], y_pairs[:-1] + z_pairs))
    ways.append((y_pairs[-1], y_pairs[-1]))

    state = [None] * len(chunks)
    done = None
    steps = len(ways) + 1
    back = [None] * len(chunks)
    result = None
    for kind, i, step in plan_of(chunks, steps):
        if kind == "node" and step == 0:
            pieces = after(received[i], done)
            state[i] = mix(pieces, coefs[0])
        elif kind == "node":
            way = ways[step - 1]
            other = [exchanged(block, axis, 2**bit) for block, (axis, bit, _) in zip(state[i], way)]
            own, other = after((state[i], other), done)
            state[i] = butterfly(own, other, tuple(pair for _, _, pair in way), coefs, step == steps - 1)
            if step == steps - 1:
                back[i] = state[i][:1] + [exchanged(state[i][d], "gz", d * stride) for d in range(1, 4)]
        elif kind == "end":
            lanes, base = (0, 1, 2, 3), None
            if i == len(chunks) - 1:
                early, lanes = (0, LANES[2], LANES[0]), LANES[1:2]
                pieces = after([back[i][d] for d in early], done)
                base = begin(pieces, early, tables)
                done = base
            pieces = after([back[i][d] for d in lanes], done)
            result = finish(pieces, lanes, base, tables, result, chunks[i][0], planes)
        done = result if kind == "end" else state[i] if kind == "node" else done
    return result


def solution(mesh):
    in_specs = (P(None, None, "gy", "gz"),)
    out_specs = P(None, None, "gy", "gz")
    return jax.shard_map(shards, mesh=mesh, in_specs=in_specs, out_specs=out_specs, check_vma=False)
```
